32 devices in a mesh: seq: 4 (over x, core), fsdp: 8 (over z, y).
Axes of the slice: x: 2, y: 2, z: 4, core: 2. Of those that a mesh axis runs over, the one named last changes fastest.
Arguments:
- hidden_in: bfloat16 [2, 8, 1536, 768], P(None, 'fsdp', 'seq'), may hold values from -6 to 6
- cotangent: bfloat16 [2, 8, 1536, 768], P(None, 'fsdp', 'seq'), may hold values from -6 to 6
- lengths: int32 [2, 8, 3], P(None, 'fsdp'), may hold values from 1 to 768, 1536 in all within a row
- slot_order: int32 [2, 8, 1536], P(None, 'fsdp'), may hold values from 0 to 1535, each once within a row
- labels: int32 [2, 8, 3], P(None, 'fsdp'), may hold values from 0 to 13
- w_qkv: bfloat16 [768, 2304], P('fsdp'), may hold values from -0.21875 to 0.21875
- bias_query: bfloat16 [768], P('fsdp'), may hold values from -1.75 to 1.75
- bias_value: bfloat16 [768], P('fsdp'), may hold values from -0.125 to 0.125
- w_out: bfloat16 [768, 768], P('fsdp'), may hold values from -3.5 to 3.5
- bias_out: bfloat16 [768], P('fsdp'), may hold values from -1.75 to 1.75
- gain_attn: bfloat16 [768], P('fsdp'), may hold values from 0.5 to 1.5
- shift_attn: bfloat16 [768], P('fsdp'), may hold values from -1.25 to 1.25
- w_up: bfloat16 [768, 3072], P('fsdp'), may hold values from -0.21875 to 0.21875
- bias_up: bfloat16 [3072], P('fsdp'), may hold values from -1.75 to 1.75
- w_down: bfloat16 [3072, 768], P('fsdp'), may hold values from -0.109375 to 0.109375
- bias_down: bfloat16 [768], P('fsdp'), may hold values from -1.75 to 1.75
- gain_ffn: bfloat16 [768], P('fsdp'), may hold values from 0.5 to 1.5
- shift_ffn: bfloat16 [768], P('fsdp'), may hold values from -1.75 to 1.75
- w_student: bfloat16 [768, 128], P('fsdp'), may hold values from -0.21875 to 0.21875
- bias_student: bfloat16 [128], P('fsdp'), may hold values from -1.75 to 1.75
- pool_query: float32 [2, 64], replicated, may hold values from -1.5 to 1.5
- w_pool: float32 [128, 128], replicated, may hold values from -1.5 to 1.5
- bias_pool: float32 [128], replicated, may hold values from -1.75 to 1.75
- w_class: float32 [128, 14], replicated, may hold values from -2 to 2
- bias_class: float32 [14], replicated, may hold values from -3 to 3
Outputs:
- hidden_out: bfloat16 [2, 8, 1536, 768], P(None, 'fsdp', 'seq')
- logits: float32 [2, 8, 3, 14], P(None, 'fsdp')
- grad_input: float32 [2, 8, 1536, 768], P(None, 'fsdp', 'seq')
- grad_w_qkv: float32 [768, 2304], P('fsdp')
- grad_bias_query: float32 [768], P('fsdp')
- grad_bias_value: float32 [768], P('fsdp')
- grad_w_out: float32 [768, 768], P('fsdp')
- grad_bias_out: float32 [768], P('fsdp')
- grad_gain_attn: float32 [768], P('fsdp')
- grad_shift_attn: float32 [768], P('fsdp')
- grad_w_up: float32 [768, 3072], P('fsdp')
- grad_bias_up: float32 [3072], P('fsdp')
- grad_w_down: float32 [3072, 768], P('fsdp')
- grad_bias_down: float32 [768], P('fsdp')
- grad_gain_ffn: float32 [768], P('fsdp')
- grad_shift_ffn: float32 [768], P('fsdp')
- grad_w_student: float32 [768, 128], P('fsdp')
- grad_bias_student: float32 [128], P('fsdp')
- grad_pool_query: float32 [2, 64], replicated
- grad_w_pool: float32 [128, 128], replicated
- grad_bias_pool: float32 [128], replicated
- grad_w_class: float32 [128, 14], replicated
- grad_bias_class: float32 [14], replicated
The draws below stay inside these ranges and needn't reach their ends.
Inputs may be any that keep to these rules, and one draw needn't show every extreme that they name: Each row of 3 lengths sums to 1536, and its largest is exactly 768. `slot_order`: each row names every number from 0 to 1535 once.
All inputs are finite; a program needn't handle non-finite values.
Results may differ from the reference program's by a relative error of at most 0.024.
The reference program's roundings to bfloat16 on the way count: a program that leaves them out, or rounds other values in their place, can miss the bound.
Values may be sent and summed in bfloat16 or wider, within the bound.
No kernel may reach another device: no remote copies, remote signals or barrier semaphores. Data moves between devices by JAX's collectives and lax.ppermute only.
A program may use at most 192 MiB of HBM per device.

```python
import math
import jax
import jax.numpy as jnp
import numpy as np
from jax import lax

D = 768
HEADS = 12
FF = 3072
HEAD_DIM = 64
STUDENT = 128
POOL_HEADS = 2
POOL_DIM = 64
CLASSES = 14
MB = 2
SEQS = 3
GRP_TOK = 1536
MAXLEN = 768
GROUPS = 8


def touch_ends(values, own_key, low, largest):
    longest = values.shape.index(max(values.shape))
    spots = []
    for shift in (0, 1):
        where = [jax.random.randint(jax.random.fold_in(own_key, axis), (), 0, length) for axis, length in enumerate(values.shape)]
        where[longest] = (where[longest] + shift) % values.shape[longest]
        spots.append(tuple(where))
    return values.at[spots[0]].set(low).at[spots[1]].set(largest)


def strengthened(values, own_key, source, target, parts, factor):
    def block_of(axis_at):
        return (jnp.arange(values.shape[axis_at]) // (values.shape[axis_at] // parts)).reshape((-1,) + (1,) * (values.ndim - 1 - axis_at))

    near = jax.random.permutation(own_key, parts)[block_of(target)]
    second = (block_of(target) + parts // 2) % parts
    return jnp.where((block_of(source) == near) | (block_of(source) == second), factor * values, values)


def level_of(rng, shape, cuts, smallest, largest):
    level = 1.0
    for axis_at, shards_of in cuts:
        draws = jax.random.uniform(jax.random.fold_in(jax.random.fold_in(rng, 6), axis_at), (shards_of,), jnp.float32, smallest / len(cuts), largest / len(cuts))
        level = level * jnp.repeat(jnp.exp(draws), shape[axis_at] // shards_of).reshape((-1,) + (1,) * (len(shape) - 1 - axis_at))
    return level


def profile(amount, total, reach, slope):
    portions = [(1 << 20) // math.isqrt(standing ** slope) + 1 for standing in range(2, amount + 1)]
    surplus, holding = total - reach - (amount - 1), [1] * (amount - 1)
    while surplus > 0:
        movable = [i for i in range(amount - 1) if holding[i] < reach]
        pool, remaining = sum([portions[i] for i in movable]), surplus
        for i in movable:
            extra = min(reach - holding[i], max(1, remaining * portions[i] // pool), surplus)
            holding[i] = holding[i] + extra
            surplus = surplus - extra
    return np.array([reach] + holding)


def uneven(rng, number_of, total, reach, lean):
    if number_of == 2:
        one = jax.random.randint(rng, (), max(1, total - reach), min(reach, total - 1) + 1)
        return jnp.stack([one, total - one])
    sizes = jnp.asarray(profile(number_of, total, reach, lean), jnp.int32)
    couples = (number_of - 1) // 2
    donor, sink = sizes[1:1 + 2 * couples:2], sizes[2:2 + 2 * couples:2]
    margin = jnp.minimum(donor - 1, reach - sink)
    moved = jax.random.randint(jax.random.fold_in(rng, 1), (couples,), 0, 1 << 20) % (margin + 1)
    sizes = sizes.at[1:1 + 2 * couples:2].set(donor - moved).at[2:2 + 2 * couples:2].set(sink + moved)
    return sizes[jax.random.permutation(jax.random.fold_in(rng, 2), number_of)]


def gaussian(own_key, shape, width, limit, cuts=(), dtype=jnp.bfloat16):
    values = jax.random.normal(own_key, shape, jnp.float32) * width
    if len(cuts) > 0:
        values = level_of(own_key, shape, cuts, -0.22, 0.18) * values
    return jnp.clip(values, min=-limit, max=limit).astype(dtype)


def noise_with(stream_key, shape, deviation, reach, split, heavy, dtype=jnp.bfloat16):
    result = deviation * jax.random.normal(stream_key, shape, jnp.float32)
    if split:
        result = result * level_of(stream_key, shape, split, -0.22, 0.18)
    return jnp.clip(strengthened(result, jax.random.fold_in(stream_key, 3), *heavy), -reach, reach).astype(dtype)


def setup_inputs(seed: int = 0) -> dict:
    arg_keys = jax.random.split(jax.random.key(seed), 26)
    return {
        "hidden_in": noise_with(arg_keys[0], (MB, GROUPS, GRP_TOK, D), 1.0, 6.0, ((1, 8), (2, 4)), (1, 3, 8, 2.0)),
        "cotangent": noise_with(arg_keys[1], (MB, GROUPS, GRP_TOK, D), 1.0, 6.0, ((1, 8), (2, 4)), (1, 3, 8, 2.0)),
        "lengths": jax.vmap(lambda own: uneven(own, SEQS, GRP_TOK, MAXLEN, 2))(jax.random.split(arg_keys[2], MB * GROUPS)).reshape((MB, GROUPS, SEQS)).astype(jnp.int32),
        "slot_order": jax.vmap(lambda own: jax.random.permutation(own, GRP_TOK))(jax.random.split(arg_keys[3], MB * GROUPS)).reshape((MB, GROUPS, GRP_TOK)).astype(jnp.int32),
        "labels": touch_ends(jax.random.randint(arg_keys[4], (MB, GROUPS, SEQS), 0, CLASSES), jax.random.fold_in(arg_keys[4], 1), 0, CLASSES - 1).astype(jnp.int32),
        "w_qkv": gaussian(arg_keys[5], (D, 3 * D), D ** -0.5, 0.21875, ((0, 8),)),
        "bias_query": gaussian(arg_keys[6], (D,), 0.3, 1.75, ((0, 8),)),
        "bias_value": gaussian(arg_keys[7], (D,), 0.02, 0.125, ((0, 8),)),
        "w_out": gaussian(arg_keys[8], (D, D), (max(2, 3 * D // MAXLEN)) ** -0.5, 3.5, ((0, 8),)),
        "bias_out": gaussian(arg_keys[9], (D,), 0.3, 1.75, ((0, 8),)),
        "gain_attn": jnp.clip(1.0 + 0.1 * jax.random.normal(arg_keys[10], (D,), jnp.float32), 0.5, 1.5).astype(jnp.bfloat16),
        "shift_attn": gaussian(arg_keys[11], (D,), 0.2, 1.25, ((0, 8),)),
        "w_up": gaussian(arg_keys[12], (D, FF), D ** -0.5, 0.21875, ((0, 8),)),
        "bias_up": gaussian(arg_keys[13], (FF,), 0.3, 1.75, ((0, 8),)),
        "w_down": gaussian(arg_keys[14], (FF, D), FF ** -0.5, 0.109375, ((0, 8),)),
        "bias_down": gaussian(arg_keys[15], (D,), 0.3, 1.75, ((0, 8),)),
        "gain_ffn": jnp.clip(1.0 + 0.1 * jax.random.normal(arg_keys[16], (D,), jnp.float32), 0.5, 1.5).astype(jnp.bfloat16),
        "shift_ffn": gaussian(arg_keys[17], (D,), 0.3, 1.75, ((0, 8),)),
        "w_student": gaussian(arg_keys[18], (D, STUDENT), D ** -0.5, 0.21875, ((0, 8),)),
        "bias_student": gaussian(arg_keys[19], (STUDENT,), 0.3, 1.75, ((0, 8),)),
        "pool_query": gaussian(arg_keys[20], (POOL_HEADS, POOL_DIM), 0.25, 1.5, (), jnp.float32),
        "w_pool": gaussian(arg_keys[21], (STUDENT, STUDENT), (STUDENT // 8) ** -0.5, 1.5, (), jnp.float32),
        "bias_pool": gaussian(arg_keys[22], (STUDENT,), 0.3, 1.75, (), jnp.float32),
        "w_class": gaussian(arg_keys[23], (STUDENT, CLASSES), (STUDENT // 16) ** -0.5, 2.0, (), jnp.float32),
        "bias_class": gaussian(arg_keys[24], (CLASSES,), 0.5, 3.0, (), jnp.float32),
    }


highest = lax.Precision.HIGHEST
masked_value = -1e+30

@jax.custom_vjp
def low(v):
    return lax.optimization_barrier(v.astype(jnp.bfloat16)).astype(jnp.float32)

@jax.custom_vjp
def low_back(v):
    return v

def low_keep(v):
    return (low(v), None)

def low_pass(kept, grad):
    return (grad,)

def back_keep(v):
    return (v, None)

def back_low(kept, grad):
    return (low(grad),)
low.defvjp(low_keep, low_pass)
low_back.defvjp(back_keep, back_low)

def matmul(left, right):
    return jnp.dot(left, right, precision=highest, preferred_element_type=jnp.float32)

def layer_norm(values, gain, shift):
    center = values - lax.optimization_barrier(jnp.mean(values, axis=-1, keepdims=True))
    spread = lax.optimization_barrier(jnp.mean(center * center, axis=-1, keepdims=True))
    return center * lax.rsqrt(spread + 1e-06) * gain + shift

def exact_gelu(values):
    return jax.nn.gelu(values, approximate=False)

def segment_ids(order_row, length_row):
    ends = jnp.cumsum(length_row).astype(jnp.int32)
    above = (order_row[:, None] >= ends[None, :-1]).astype(jnp.int32)
    return lax.optimization_barrier(jnp.sum(above, axis=1)).astype(jnp.int32)

def to_heads(values):
    return values.reshape(GRP_TOK, HEADS, HEAD_DIM).transpose(1, 0, 2)

def attention(query, key_rows, value_rows, segment):
    block_rows = min(512, GRP_TOK)
    blocks = GRP_TOK // block_rows
    query_blocks = query.reshape(HEADS, blocks, block_rows, HEAD_DIM).transpose(1, 0, 2, 3)
    segment_blocks = segment.reshape(blocks, block_rows)
    scaling = HEAD_DIM ** (-0.5)

    @jax.checkpoint
    def one_block(inputs):
        query_part, segment_part = inputs
        scores = jnp.einsum('hqd,hkd->hqk', query_part, key_rows, precision=highest) * scaling
        scores = low_back(scores)
        same_doc = (segment_part[:, None] == segment[None, :])[None]
        scores = jnp.where(same_doc, scores, masked_value)
        row_peak = lax.optimization_barrier(jnp.max(scores, axis=-1, keepdims=True))
        exponent = jnp.exp(scores - row_peak)
        probs = low(exponent / lax.optimization_barrier(jnp.sum(exponent, axis=-1, keepdims=True)))
        return jnp.einsum('hqk,hkd->hqd', probs, value_rows, precision=highest)
    block_out = lax.map(one_block, (query_blocks, segment_blocks))
    return block_out.transpose(1, 0, 2, 3).reshape(HEADS, GRP_TOK, HEAD_DIM)

def pooling(student, segment, pool_query):
    members = (segment[:, None] == jnp.arange(SEQS)[None, :])[:, :, None]
    pieces = student.reshape(GRP_TOK, POOL_HEADS, POOL_DIM)
    energy = lax.optimization_barrier(jnp.sum(pieces * pool_query[None], axis=-1))
    row_peak = lax.optimization_barrier(jnp.max(jnp.where(members, energy[:, None, :], masked_value), axis=0))
    weights = jnp.exp(jnp.where(members, energy[:, None, :] - row_peak[None], masked_value))
    totals = lax.optimization_barrier(jnp.sum(weights, axis=0))
    summed = jnp.einsum('tnh,thd->nhd', weights, pieces, precision=highest)
    return (summed / totals[:, :, None]).reshape(SEQS, STUDENT)

def classify(pooled, w_pool, bias_pool, w_class, bias_class, labels):
    inner = jnp.tanh(jnp.dot(pooled, w_pool, precision=highest, preferred_element_type=jnp.float32) + bias_pool)
    logits = jnp.dot(inner, w_class, precision=highest, preferred_element_type=jnp.float32) + bias_class
    row_peak = lax.optimization_barrier(jnp.max(logits, axis=-1, keepdims=True))
    log_total = row_peak[:, 0] + jnp.log(lax.optimization_barrier(jnp.sum(jnp.exp(logits - row_peak), axis=-1)))
    classes = jnp.arange(logits.shape[1])
    picked = lax.optimization_barrier(jnp.sum(jnp.where(classes[None, :] == labels[:, None], logits, 0.0), axis=-1))
    return (jnp.sum(log_total - picked), logits)

def group_forward(params, hidden, segment, cotangent_rows, label_row):
    w_qkv, bias_query, bias_value, w_out, bias_out, gain_attn, shift_attn, w_up, bias_up, w_down, bias_down, gain_ffn, shift_ffn, w_student, bias_student, pool_query, w_pool, bias_pool, w_class, bias_class = params
    projected = matmul(hidden, w_qkv)
    query = low(low_back(projected[:, :D] + bias_query))
    key_rows = low(low_back(projected[:, D:2 * D]))
    value_rows = low(low_back(projected[:, 2 * D:] + bias_value))
    heads_out = attention(to_heads(query), to_heads(key_rows), to_heads(value_rows), segment)
    context = low(low_back(heads_out.transpose(1, 0, 2).reshape(GRP_TOK, D)))
    branch = low_back(matmul(context, w_out) + bias_out)
    normed = layer_norm(hidden + branch, gain_attn, shift_attn)
    upward = low_back(matmul(low(normed), w_up) + bias_up)
    active = low(exact_gelu(upward))
    downward = low_back(matmul(active, w_down) + bias_down)
    final = layer_norm(normed + downward, gain_ffn, shift_ffn)
    student = low_back(matmul(low(final), w_student) + bias_student)
    pooled = pooling(student, segment, pool_query)
    head_loss, logits = classify(pooled, w_pool, bias_pool, w_class, bias_class, label_row)
    return (jnp.sum(final * cotangent_rows) + head_loss, (final, logits))

def reference(hidden_in, cotangent, lengths, slot_order, labels, w_qkv, bias_query, bias_value, w_out, bias_out, gain_attn, shift_attn, w_up, bias_up, w_down, bias_down, gain_ffn, shift_ffn, w_student, bias_student, pool_query, w_pool, bias_pool, w_class, bias_class):
    params = tuple((array.astype(jnp.float32) for array in (w_qkv, bias_query, bias_value, w_out, bias_out, gain_attn, shift_attn, w_up, bias_up, w_down, bias_down, gain_ffn, shift_ffn, w_student, bias_student, pool_query, w_pool, bias_pool, w_class, bias_class)))
    hidden_all = hidden_in.astype(jnp.float32).reshape(MB * GROUPS, GRP_TOK, D)
    cotangent_all = cotangent.astype(jnp.float32).reshape(MB * GROUPS, GRP_TOK, D)
    length_all = lengths.reshape(MB * GROUPS, SEQS)
    order_all = slot_order.reshape(MB * GROUPS, GRP_TOK)
    label_all = labels.reshape(MB * GROUPS, SEQS)

    def one_group(totals, inputs):
        hidden, cotangent_rows, length_row, order_row, label_row = inputs
        segment = segment_ids(order_row, length_row)

        def objective(weights, hidden_rows):
            return group_forward(weights, hidden_rows, segment, cotangent_rows, label_row)
        loss, back_fn, (final, logits) = jax.vjp(objective, params, hidden, has_aux=True)
        grad_params, grad_hidden = back_fn(jnp.ones_like(loss))
        totals = jax.tree.map(jnp.add, totals, grad_params)
        return (totals, (final.astype(jnp.bfloat16), logits, grad_hidden))
    zeros = jax.tree.map(jnp.zeros_like, params)
    totals, (finals, logits, grad_hidden) = lax.scan(one_group, zeros, (hidden_all, cotangent_all, length_all, order_all, label_all))
    return (finals.reshape(MB, GROUPS, GRP_TOK, D), logits.reshape(MB, GROUPS, SEQS, CLASSES), grad_hidden.reshape(MB, GROUPS, GRP_TOK, D), totals[0], totals[1], totals[2], totals[3], totals[4], totals[5], totals[6], totals[7], totals[8], totals[9], totals[10], totals[11], totals[12], totals[13], totals[14], totals[15], totals[16], totals[17], totals[18], totals[19])
```

```python
import jax
import jax.numpy as jnp
from jax import lax
from jax.sharding import PartitionSpec as P

HEAD_DIM = 64
highest = lax.Precision.HIGHEST
masked_value = -1e30
bf16 = jnp.bfloat16
f32 = jnp.float32


def factors(count):
    found = []
    while count % 4 == 0:
        found.append(4)
        count //= 4
    if count > 1:
        found.append(count)
    return sorted(found)


def ring_pairs(count, stride, radix):
    pairs = []
    for source in range(count):
        digit = (source // stride) % radix
        pairs.append((source, source + ((digit + 1) % radix - digit) * stride))
    return pairs


def swap(value, mask):
    count = lax.axis_size("seq")
    return lax.ppermute(value, "seq", [(i, i ^ mask) for i in range(count)])


def pair_stack(value, mask, bit, axis):
    other = swap(value, mask)
    return jnp.stack([jnp.where(bit == 0, value, other), jnp.where(bit == 0, other, value)], axis)


def ring_gather(value):
    count = lax.axis_size("fsdp")
    index = lax.axis_index("fsdp")
    total = value[None]
    stride = 1
    for radix in factors(count):
        digit = (index // stride) % radix
        pairs = ring_pairs(count, stride, radix)
        current = total
        parts = [total]
        for _ in range(radix - 1):
            current = lax.ppermute(current, "fsdp", pairs)
            parts.append(current)
        if radix == 2:
            stacked = jnp.stack(
                [jnp.where(digit == 0, parts[0], parts[1]), jnp.where(digit == 0, parts[1], parts[0])]
            )
        else:
            stacked = jnp.zeros((radix,) + total.shape, total.dtype)
            for step, part in enumerate(parts):
                stacked = lax.dynamic_update_index_in_dim(
                    stacked, part, lax.rem(digit - step + radix, radix), 0
                )
        total = stacked.reshape((radix * total.shape[0],) + value.shape)
        stride *= radix
    return total


def ring_scatter(value, wire=bf16):
    count = lax.axis_size("fsdp")
    index = lax.axis_index("fsdp")
    stride = 1
    for radix in factors(count):
        digit = (index // stride) % radix
        pairs = ring_pairs(count, stride, radix)
        view = value.reshape((value.shape[0] // radix, radix) + value.shape[1:])

        def own(offset):
            return lax.dynamic_index_in_dim(
                view, lax.rem(digit + offset + 2 * radix, radix), 1, keepdims=False
            )

        current = own(-1)
        for step in range(radix - 1):
            moved = lax.ppermute(current.astype(wire), "fsdp", pairs)
            current = own(-2 - step) + moved.astype(f32)
        value = current
        stride *= radix
    return value[0]


def ring_sum(value):
    count = lax.axis_size("fsdp")
    stride = 1
    for radix in factors(count):
        pairs = ring_pairs(count, stride, radix)
        index = (lax.axis_index("fsdp") // stride) % radix
        current = value
        parts = [value]
        for _ in range(radix - 1):
            current = lax.ppermute(current, "fsdp", pairs)
            parts.append(current)
        if radix == 2:
            value = parts[0] + parts[1]
        else:
            stacked = jnp.zeros((radix,) + value.shape, value.dtype)
            for step, part in enumerate(parts):
                stacked = lax.dynamic_update_index_in_dim(
                    stacked, part, lax.rem(index - step + radix, radix), 0
                )
            value = jnp.sum(stacked, axis=0)
        stride *= radix
    return value


def seq_sum(value, wire=f32):
    value = value + swap(value.astype(wire), 1).astype(f32)
    return value + swap(value.astype(wire), 2).astype(f32)


def by_seq(parts, chip, core):
    first = [
        jnp.where(core == 0, parts[0], parts[1]),
        jnp.where(core == 0, parts[1], parts[0]),
        jnp.where(core == 0, parts[2], parts[3]),
        jnp.where(core == 0, parts[3], parts[2]),
    ]
    return [
        jnp.where(chip == 0, first[0], first[2]),
        jnp.where(chip == 0, first[1], first[3]),
        jnp.where(chip == 0, first[2], first[0]),
        jnp.where(chip == 0, first[3], first[1]),
    ]


def gather_rows(shard, core):
    rows, columns = shard.shape
    half = rows // 2
    mine = lax.dynamic_slice_in_dim(shard, core * half, half)
    gathered = ring_gather(mine)
    return pair_stack(gathered, 1, core, 1).reshape(-1, columns)


def reduce_rows(grad, chip, core):
    rows, columns = grad.shape
    count = lax.axis_size("fsdp")
    half = rows // (2 * count)
    wide = columns // 2
    view = grad.reshape(count, 2, half, 2, wide)
    sent = lax.dynamic_index_in_dim(view, 1 - core, 1, keepdims=False).astype(bf16)
    kept = lax.dynamic_index_in_dim(view, core, 1, keepdims=False)
    kept = kept + swap(sent, 1).astype(f32)
    sent = lax.dynamic_index_in_dim(kept, 1 - chip, 2, keepdims=False).astype(bf16)
    kept = lax.dynamic_index_in_dim(kept, chip, 2, keepdims=False)
    kept = kept + swap(sent, 2).astype(f32)
    owned = ring_scatter(kept).astype(bf16)
    both = pair_stack(owned, 2, chip, 1)
    return pair_stack(both, 1, core, 0).reshape(2 * half, columns).astype(f32)


def layer_norm(values, gain, shift):
    center = values - jnp.mean(values, axis=-1, keepdims=True)
    spread = jnp.mean(center * center, axis=-1, keepdims=True)
    return center * lax.rsqrt(spread + 1e-06) * gain + shift


def exact_gelu(values):
    return jax.nn.gelu(values, approximate=False)


def segment_ids(order_row, length_row):
    ends = jnp.cumsum(length_row)
    above = (order_row[:, None] >= ends[None, :-1]).astype(jnp.int32)
    return jnp.sum(above, axis=1)


def classify(pooled, w_pool, bias_pool, w_class, bias_class, labels):
    inner = jnp.tanh(
        jnp.dot(pooled, w_pool, precision=highest, preferred_element_type=f32) + bias_pool
    )
    logits = jnp.dot(inner, w_class, precision=highest, preferred_element_type=f32) + bias_class
    row_peak = jnp.max(logits, axis=-1, keepdims=True)
    log_total = row_peak[:, 0] + jnp.log(jnp.sum(jnp.exp(logits - row_peak), axis=-1))
    classes = jnp.arange(logits.shape[1])
    picked = jnp.sum(jnp.where(classes[None, :] == labels[:, None], logits, 0.0), axis=-1)
    return (jnp.sum(log_total - picked), logits)


def big_product(left, right):
    return jnp.dot(left, right, preferred_element_type=f32)


def left_product(left, right):
    return lax.dot_general(left, right, (((0,), (0,)), ((), ())), preferred_element_type=f32)


def right_product(left, right):
    return lax.dot_general(left, right, (((1,), (1,)), ((), ())), preferred_element_type=f32)


def combine_parts(first, second):
    new_peak = jnp.maximum(first[0], second[0])
    first_scale = jnp.exp(first[0] - new_peak)
    second_scale = jnp.exp(second[0] - new_peak)
    return (
        new_peak,
        first[1] * first_scale + second[1] * second_scale,
        first[2] * first_scale[..., None] + second[2] * second_scale[..., None],
    )


def attention_forward(query, key, value, segments):
    tokens, width = query.shape
    heads = width // HEAD_DIM
    scaling = HEAD_DIM ** (-0.5)
    rows = min(512, tokens)
    blocks = tokens // rows
    key_all = key.reshape(tokens, heads, HEAD_DIM)
    value_all = value.reshape(tokens, heads, HEAD_DIM)

    def one_block(inputs):
        query_part, segment_part = inputs
        scores = jnp.einsum("qhd,khd->hqk", query_part, key_all, preferred_element_type=f32)
        same = (segment_part[:, None] == segments[None, :])[None]
        scores = jnp.where(same, scores * scaling, masked_value)
        peak = jnp.max(scores, axis=-1, keepdims=True)
        exponent = jnp.exp(scores - peak)
        totals = jnp.sum(exponent, axis=-1, keepdims=True)
        probs = (exponent / totals).astype(bf16)
        context = jnp.einsum("hqk,khd->qhd", probs, value_all, preferred_element_type=f32)
        return (context.astype(bf16), peak[:, :, 0] + jnp.log(totals[:, :, 0]))

    contexts, logs = lax.map(
        one_block,
        (query.reshape(blocks, rows, heads, HEAD_DIM), segments.reshape(blocks, rows)),
    )
    return contexts.reshape(tokens, width), logs


def attention_backward(query, key, value, segments, logs, grad_context):
    tokens, width = query.shape
    heads = width // HEAD_DIM
    scaling = HEAD_DIM ** (-0.5)
    rows = min(512, tokens)
    blocks = tokens // rows
    key_all = key.reshape(tokens, heads, HEAD_DIM)
    value_all = value.reshape(tokens, heads, HEAD_DIM)

    def one_block(carry, inputs):
        query_part, segment_part, log_part, grad_part = inputs
        scores = jnp.einsum("qhd,khd->hqk", query_part, key_all, preferred_element_type=f32)
        same = (segment_part[:, None] == segments[None, :])[None]
        soft = jnp.exp(jnp.where(same, scores * scaling, masked_value) - log_part[:, :, None])
        grad_soft = jnp.einsum("qhd,khd->hqk", grad_part, value_all, preferred_element_type=f32)
        inner = jnp.sum(soft * grad_soft, axis=-1, keepdims=True)
        grad_scores = (soft * (grad_soft - inner)).astype(bf16)
        grad_query = (
            jnp.einsum("hqk,khd->qhd", grad_scores, key_all, preferred_element_type=f32) * scaling
        )
        grad_key = carry[0] + scaling * jnp.einsum(
            "hqk,qhd->khd", grad_scores, query_part, preferred_element_type=f32
        )
        grad_value = carry[1] + jnp.einsum(
            "hqk,qhd->khd", soft.astype(bf16), grad_part, preferred_element_type=f32
        )
        return ((grad_key, grad_value), grad_query.astype(bf16))

    zeros = jnp.zeros((tokens, heads, HEAD_DIM), f32)
    (grad_key, grad_value), grad_query = lax.scan(
        one_block,
        (zeros, zeros),
        (
            query.reshape(blocks, rows, heads, HEAD_DIM),
            segments.reshape(blocks, rows),
            logs,
            grad_context.reshape(blocks, rows, heads, HEAD_DIM),
        ),
    )
    return jnp.concatenate(
        [
            grad_query.reshape(tokens, width),
            grad_key.astype(bf16).reshape(tokens, width),
            grad_value.astype(bf16).reshape(tokens, width),
        ],
        axis=1,
    )


def body(
    hidden_in,
    cotangent,
    lengths,
    slot_order,
    labels,
    w_qkv,
    bias_query,
    bias_value,
    w_out,
    bias_out,
    gain_attn,
    shift_attn,
    w_up,
    bias_up,
    w_down,
    bias_down,
    gain_ffn,
    shift_ffn,
    w_student,
    bias_student,
    pool_query,
    w_pool,
    bias_pool,
    w_class,
    bias_class,
):
    seq_count = lax.axis_size("seq")
    fsdp_count = lax.axis_size("fsdp")
    seq_index = lax.axis_index("seq")
    chip = seq_index // 2
    core = seq_index % 2
    micro = hidden_in.shape[0]
    tokens = hidden_in.shape[2]
    width = hidden_in.shape[3]
    group = slot_order.shape[2]
    docs = lengths.shape[2]
    pool_heads, pool_dim = pool_query.shape
    head_width = width // seq_count
    shard = w_qkv.shape[0]
    first_seq = (seq_index == 0).astype(f32)

    small_list = (
        bias_query,
        bias_value,
        bias_out,
        gain_attn,
        shift_attn,
        bias_up,
        bias_down,
        gain_ffn,
        shift_ffn,
        bias_student,
        w_student.reshape(-1),
    )
    small_all = ring_gather(jnp.concatenate(small_list))
    full_small = []
    start = 0
    for part in small_list:
        size = part.shape[0]
        full_small.append(small_all[:, start : start + size].reshape(-1))
        start += size
    (
        full_bias_query,
        full_bias_value,
        full_bias_out,
        full_gain_attn,
        full_shift_attn,
        full_bias_up,
        full_bias_down,
        full_gain_ffn,
        full_shift_ffn,
        full_bias_student,
    ) = [part.astype(f32) for part in full_small[:-1]]
    full_student = full_small[-1].reshape(width, -1)

    own_qkv_shard = lax.dynamic_index_in_dim(
        w_qkv.reshape(shard, 3, seq_count, head_width), seq_index, 2, keepdims=False
    ).reshape(shard, 3 * head_width)
    own_qkv = ring_gather(own_qkv_shard).reshape(width, 3 * head_width)
    own_bias = jnp.concatenate(
        [
            lax.dynamic_slice_in_dim(full_bias_query, seq_index * head_width, head_width),
            jnp.zeros((head_width,), f32),
            lax.dynamic_slice_in_dim(full_bias_value, seq_index * head_width, head_width),
        ]
    )

    hidden = hidden_in[:, 0]
    full_hidden = []
    for m in range(micro):
        both = pair_stack(hidden[m], 2, chip, 0)
        full_hidden.append(pair_stack(both, 1, core, 1).reshape(group, width))

    full_out = gather_rows(w_out, core)
    full_up = gather_rows(w_up, core)
    full_down = gather_rows(w_down, core)

    segments = [segment_ids(slot_order[m, 0], lengths[m, 0]) for m in range(micro)]

    saved = []
    context_parts = []
    for m in range(micro):
        projected = (big_product(full_hidden[m], own_qkv) + own_bias).astype(bf16)
        query = projected[:, :head_width]
        key = projected[:, head_width : 2 * head_width]
        value = projected[:, 2 * head_width :]
        context_own, logs = attention_forward(query, key, value, segments[m])
        saved.append((query, key, value, logs))
        view = context_own.reshape(seq_count, tokens, head_width)
        parts = []
        for mask in range(seq_count):
            part = lax.dynamic_index_in_dim(view, seq_index ^ mask, 0, keepdims=False)
            parts.append(part if mask == 0 else swap(part, mask))
        context_parts.append(jnp.concatenate(parts, axis=1))
    context = jnp.concatenate(context_parts, axis=0)
    out_view = full_out.reshape(seq_count, head_width, width)
    out_turned = jnp.concatenate(
        [
            lax.dynamic_index_in_dim(out_view, seq_index ^ mask, 0, keepdims=False)
            for mask in range(seq_count)
        ],
        axis=0,
    )
    branch = big_product(context, out_turned) + full_bias_out
    hidden_rows = hidden.reshape(micro * tokens, width)
    normed, first_norm_back = jax.vjp(
        layer_norm, hidden_rows.astype(f32) + branch, full_gain_attn, full_shift_attn
    )
    normed_low = normed.astype(bf16)
    upward = big_product(normed_low, full_up) + full_bias_up
    active, gelu_back = jax.vjp(exact_gelu, upward)
    active_low = active.astype(bf16)
    downward = big_product(active_low, full_down) + full_bias_down
    final, second_norm_back = jax.vjp(
        layer_norm, normed + downward, full_gain_ffn, full_shift_ffn
    )
    final_low = final.astype(bf16)

    student = big_product(final_low, full_student) + full_bias_student
    pieces = student.reshape(micro, tokens, pool_heads, pool_dim)
    energy = jnp.sum(pieces * pool_query, axis=-1)
    segment_local = jnp.stack(
        [lax.dynamic_slice_in_dim(part, seq_index * tokens, tokens) for part in segments]
    )
    members = (segment_local[:, :, None] == jnp.arange(docs, dtype=jnp.int32))[..., None]
    local_peak = jnp.max(jnp.where(members, energy[:, :, None, :], masked_value), axis=1)
    local_weights = jnp.exp(
        jnp.where(members, energy[:, :, None, :] - local_peak[:, None], masked_value)
    )
    local_total = jnp.sum(local_weights, axis=1)
    local_accum = jnp.einsum("btnh,bthd->bnhd", local_weights, pieces, precision=highest)
    packed = jnp.concatenate([local_peak[..., None], local_total[..., None], local_accum], axis=-1)
    for mask in (1, 2):
        other = swap(packed, mask)
        peak, total, accum = combine_parts(
            (packed[..., 0], packed[..., 1], packed[..., 2:]),
            (other[..., 0], other[..., 1], other[..., 2:]),
        )
        packed = jnp.concatenate([peak[..., None], total[..., None], accum], axis=-1)
    global_peak, global_total, global_accum = packed[..., 0], packed[..., 1], packed[..., 2:]
    pooled_heads = global_accum / global_total[..., None]
    pooled = pooled_heads.reshape(micro * docs, -1)

    def head_loss(pooled_rows, pool_weight, pool_bias, class_weight, class_bias):
        return classify(
            pooled_rows, pool_weight, pool_bias, class_weight, class_bias, labels.reshape(-1)
        )

    loss_value, head_back, logit_rows = jax.vjp(
        head_loss, pooled, w_pool, bias_pool, w_class, bias_class, has_aux=True
    )
    logits = logit_rows.reshape(micro, 1, docs, -1)
    grad_pooled, grad_wpool, grad_bpool, grad_wclass, grad_bclass = head_back(
        jnp.ones_like(loss_value)
    )
    alpha = (
        jnp.exp(jnp.where(members, energy[:, :, None, :] - global_peak[:, None], masked_value))
        / global_total[:, None]
    )
    grad_heads = grad_pooled.reshape(micro, docs, pool_heads, pool_dim)
    along = jnp.einsum("bthd,bnhd->btnh", pieces, grad_heads, precision=highest)
    baseline = jnp.sum(pooled_heads * grad_heads, axis=-1)
    grad_energy = jnp.sum(alpha * (along - baseline[:, None]), axis=2)
    grad_pieces = (
        jnp.einsum("btnh,bnhd->bthd", alpha, grad_heads, precision=highest)
        + grad_energy[..., None] * pool_query
    )
    grad_pool_query = jnp.einsum("bth,bthd->hd", grad_energy, pieces, precision=highest)
    grad_student = grad_pieces.reshape(micro * tokens, -1).astype(bf16)
    grad_w_student = left_product(final_low, grad_student)
    grad_bias_student = jnp.sum(grad_student.astype(f32), axis=0)

    cotangent_rows = cotangent[:, 0].reshape(micro * tokens, width)
    grad_final = cotangent_rows.astype(f32) + right_product(grad_student, full_student)
    grad_mid, grad_gain_ffn, grad_shift_ffn = second_norm_back(grad_final)
    grad_down = grad_mid.astype(bf16)
    grad_bias_down = jnp.sum(grad_down.astype(f32), axis=0)
    grad_w_down = left_product(active_low, grad_down)
    (grad_upward,) = gelu_back(right_product(grad_down, full_down))
    grad_up = grad_upward.astype(bf16)
    grad_bias_up = jnp.sum(grad_up.astype(f32), axis=0)
    grad_w_up = left_product(normed_low, grad_up)
    grad_normed = grad_mid + right_product(grad_up, full_up)
    grad_res, grad_gain_attn, grad_shift_attn = first_norm_back(grad_normed)
    grad_branch = grad_res.astype(bf16)
    grad_bias_out = jnp.sum(grad_branch.astype(f32), axis=0)
    grad_out_turned = left_product(context, grad_branch).reshape(seq_count, head_width, width)
    grad_w_out = jnp.concatenate(
        by_seq([grad_out_turned[m] for m in range(seq_count)], chip, core), axis=0
    )
    grad_context = right_product(grad_branch, out_turned).astype(bf16)

    grad_own_qkv = None
    grad_bias_own = None
    grad_inputs = []
    for m in range(micro):
        rows = grad_context[m * tokens : (m + 1) * tokens]
        parts = []
        for mask in range(seq_count):
            part = rows[:, mask * head_width : (mask + 1) * head_width]
            parts.append(part if mask == 0 else swap(part, mask))
        grad_context_own = jnp.concatenate(by_seq(parts, chip, core), axis=0)
        query, key, value, logs = saved[m]
        grad_proj = attention_backward(query, key, value, segments[m], logs, grad_context_own)
        bias_sum = jnp.sum(grad_proj.astype(f32), axis=0)
        weight_sum = left_product(full_hidden[m], grad_proj)
        grad_bias_own = bias_sum if grad_bias_own is None else grad_bias_own + bias_sum
        grad_own_qkv = weight_sum if grad_own_qkv is None else grad_own_qkv + weight_sum
        partial = right_product(grad_proj, own_qkv).reshape(2, 2, tokens, width)
        sent = lax.dynamic_index_in_dim(partial, 1 - core, 1, keepdims=False).astype(bf16)
        kept = lax.dynamic_index_in_dim(partial, core, 1, keepdims=False)
        kept = kept + swap(sent, 1).astype(f32)
        sent = lax.dynamic_index_in_dim(kept, 1 - chip, 0, keepdims=False).astype(bf16)
        kept = lax.dynamic_index_in_dim(kept, chip, 0, keepdims=False)
        kept = kept + swap(sent, 2).astype(f32)
        grad_inputs.append(grad_res[m * tokens : (m + 1) * tokens] + kept)

    out_w_down = reduce_rows(grad_w_down, chip, core)
    out_w_up = reduce_rows(grad_w_up, chip, core)
    out_w_out = reduce_rows(grad_w_out, chip, core)
    owned_qkv = ring_scatter(grad_own_qkv.reshape(fsdp_count, shard, 3 * head_width)).astype(bf16)
    both = pair_stack(owned_qkv.reshape(shard, 3, head_width), 2, chip, 2)
    out_w_qkv = pair_stack(both, 1, core, 3).reshape(shard, 3 * width).astype(f32)

    early = (
        grad_bias_out,
        grad_gain_attn,
        grad_shift_attn,
        grad_bias_up,
        grad_bias_down,
        grad_gain_ffn,
        grad_shift_ffn,
        grad_bias_student,
        grad_w_student.reshape(-1),
    )
    early_packed = jnp.concatenate([part.reshape(fsdp_count, -1) for part in early], axis=1)
    early_owned = ring_scatter(seq_sum(early_packed, bf16))
    placed_bias = jnp.zeros((2, seq_count, head_width), f32)
    placed_bias = lax.dynamic_update_slice(
        placed_bias,
        grad_bias_own.reshape(3, 1, head_width)[::2],
        (0, seq_index, 0),
    ).reshape(2, fsdp_count, -1)
    late_packed = jnp.concatenate([placed_bias[0], placed_bias[1]], axis=1)
    late_owned = ring_scatter(seq_sum(late_packed), f32)
    early_out = []
    start = 0
    for part in early:
        size = part.size // fsdp_count
        early_out.append(early_owned[start : start + size])
        start += size
    bias_size = late_owned.shape[0] // 2

    query_total = seq_sum(grad_pool_query)
    head_list = (query_total, grad_wpool, grad_bpool, grad_wclass, grad_bclass)
    head_packed = ring_sum(jnp.concatenate([part.reshape(-1) for part in head_list]))
    head_out = []
    start = 0
    for part in head_list:
        head_out.append(head_packed[start : start + part.size].reshape(part.shape))
        start += part.size

    return (
        final_low.reshape(micro, 1, tokens, width),
        logits,
        jnp.stack(grad_inputs)[:, None],
        out_w_qkv,
        late_owned[:bias_size],
        late_owned[bias_size:],
        out_w_out,
        early_out[0],
        early_out[1],
        early_out[2],
        out_w_up,
        early_out[3],
        out_w_down,
        early_out[4],
        early_out[5],
        early_out[6],
        early_out[8].reshape(w_student.shape),
        early_out[7],
    ) + tuple(head_out)


def solution(mesh):
    rows, vector = P("fsdp", None), P("fsdp")
    sharded = (
        rows, vector, vector, rows, vector, vector, vector, rows,
        vector, rows, vector, vector, vector, rows, vector,
    )
    return jax.shard_map(
        body,
        mesh=mesh,
        in_specs=(P(None, "fsdp", "seq", None),) * 2
        + (P(None, "fsdp", None),) * 3
        + sharded
        + (P(),) * 5,
        out_specs=(
            P(None, "fsdp", "seq", None),
            P(None, "fsdp", None, None),
            P(None, "fsdp", "seq", None),
        )
        + sharded
        + (P(),) * 5,
        check_vma=False,
    )
```

```python
import functools

import jax
import jax.numpy as jnp
from jax import lax
from jax.experimental import pallas as pl
from jax.experimental.pallas import tpu as pltpu
from jax.sharding import PartitionSpec as P

HEAD_DIM = 64
highest = lax.Precision.HIGHEST
masked_value = -1e30
bf16 = jnp.bfloat16
f32 = jnp.float32


def factors(count):
    found = []
    while count % 4 == 0:
        found.append(4)
        count //= 4
    if count > 1:
        found.append(count)
    return sorted(found)


def ring_pairs(count, stride, radix, shift):
    pairs = []
    for source in range(count):
        digit = (source // stride) % radix
        pairs.append((source, source + ((digit + shift) % radix - digit) * stride))
    return pairs


def swap(value, mask):
    count = lax.axis_size("seq")
    return lax.ppermute(value, "seq", [(i, i ^ mask) for i in range(count)])


def pair_stack(value, mask, bit, axis):
    other = swap(value, mask)
    return jnp.stack([jnp.where(bit == 0, value, other), jnp.where(bit == 0, other, value)], axis)


def strides(count):
    found = []
    stride = 1
    for radix in factors(count):
        found.append((radix, stride))
        stride *= radix
    return found


def digit_gather(total, radix, stride, axis):
    count = lax.axis_size("fsdp")
    digit = (lax.axis_index("fsdp") // stride) % radix
    parts = [total] + [
        lax.ppermute(total, "fsdp", ring_pairs(count, stride, radix, shift))
        for shift in range(1, radix)
    ]
    if radix == 2:
        return jnp.stack(
            [jnp.where(digit == 0, parts[0], parts[1]), jnp.where(digit == 0, parts[1], parts[0])],
            axis,
        )
    shape = total.shape[:axis] + (radix,) + total.shape[axis:]
    stacked = jnp.zeros(shape, total.dtype)
    for shift, part in enumerate(parts):
        stacked = lax.dynamic_update_index_in_dim(
            stacked, part, lax.rem(digit - shift + radix, radix), axis
        )
    return stacked


def ring_gather(value):
    total = value[None]
    for radix, stride in reversed(strides(lax.axis_size("fsdp"))):
        total = digit_gather(total, radix, stride, 1)
        total = total.reshape((-1,) + value.shape)
    return total


def digit_scatter(value, radix, stride, wire):
    count = lax.axis_size("fsdp")
    digit = (lax.axis_index("fsdp") // stride) % radix
    view = value.reshape((value.shape[0] // radix, radix) + value.shape[1:])

    def piece(offset):
        return lax.dynamic_index_in_dim(view, lax.rem(digit + offset, radix), 1, keepdims=False)

    total = piece(0)
    for shift in range(1, radix):
        moved = lax.ppermute(
            piece(shift).astype(wire), "fsdp", ring_pairs(count, stride, radix, shift)
        )
        total = total + moved.astype(f32)
    return total


def ring_scatter(value, wire=bf16):
    for radix, stride in strides(lax.axis_size("fsdp")):
        value = digit_scatter(value, radix, stride, wire)
    return value[0]


def ring_sum(value):
    for radix, stride in strides(lax.axis_size("fsdp")):
        value = jnp.sum(digit_gather(value, radix, stride, 0), axis=0)
    return value


def seq_sum(value, wire=f32):
    value = value + swap(value.astype(wire), 1).astype(f32)
    return value + swap(value.astype(wire), 2).astype(f32)


def by_seq(parts, chip, core):
    first = [
        jnp.where(core == 0, parts[0], parts[1]),
        jnp.where(core == 0, parts[1], parts[0]),
        jnp.where(core == 0, parts[2], parts[3]),
        jnp.where(core == 0, parts[3], parts[2]),
    ]
    return [
        jnp.where(chip == 0, first[0], first[2]),
        jnp.where(chip == 0, first[1], first[3]),
        jnp.where(chip == 0, first[2], first[0]),
        jnp.where(chip == 0, first[3], first[1]),
    ]


def gather_rows(shard, core):
    rows, columns = shard.shape
    half = rows // 2
    mine = lax.dynamic_slice_in_dim(shard, core * half, half)
    gathered = ring_gather(mine)
    return pair_stack(gathered, 1, core, 1).reshape(-1, columns)


def core_stage(grad, chip, core):
    rows, columns = grad.shape
    count = lax.axis_size("fsdp")
    half = rows // (2 * count)
    wide = columns // 2
    view = grad.reshape(count, 2, half, columns)
    other = lax.dynamic_index_in_dim(view, 1 - core, 1, keepdims=False).astype(bf16)
    total = lax.dynamic_index_in_dim(view, core, 1, keepdims=False) + swap(other, 1).astype(f32)
    low, high = total[..., :wide], total[..., wide:]
    return jnp.where(chip == 0, low, high), jnp.where(chip == 0, high, low).astype(bf16)


def chip_stage(pair):
    kept, sent = pair
    return kept + swap(sent, 2).astype(f32)


def collect(owned, chip, core):
    both = pair_stack(owned.astype(bf16), 2, chip, 0)
    both = jnp.concatenate([both[0], both[1]], axis=-1)
    return pair_stack(both, 1, core, 0).reshape(-1, both.shape[-1]).astype(f32)


def small_stages(value):
    for radix, stride in strides(lax.axis_size("fsdp"))[:-1]:
        value = digit_scatter(value, radix, stride, bf16)
    return value


def last_stage(value):
    radix, stride = strides(lax.axis_size("fsdp"))[-1]
    return digit_scatter(value, radix, stride, bf16)[0]


def layer_norm(values, gain, shift):
    center = values - jnp.mean(values, axis=-1, keepdims=True)
    spread = jnp.mean(center * center, axis=-1, keepdims=True)
    return center * lax.rsqrt(spread + 1e-06) * gain + shift


def exact_gelu(values):
    return jax.nn.gelu(values, approximate=False)


def segment_ids(order_row, length_row):
    ends = jnp.cumsum(length_row)
    above = (order_row[:, None] >= ends[None, :-1]).astype(jnp.int32)
    return jnp.sum(above, axis=1)


def classify(pooled, w_pool, bias_pool, w_class, bias_class, labels):
    inner = jnp.tanh(
        jnp.dot(pooled, w_pool, precision=highest, preferred_element_type=f32) + bias_pool
    )
    logits = jnp.dot(inner, w_class, precision=highest, preferred_element_type=f32) + bias_class
    row_peak = jnp.max(logits, axis=-1, keepdims=True)
    log_total = row_peak[:, 0] + jnp.log(jnp.sum(jnp.exp(logits - row_peak), axis=-1))
    classes = jnp.arange(logits.shape[1])
    picked = jnp.sum(jnp.where(classes[None, :] == labels[:, None], logits, 0.0), axis=-1)
    return (jnp.sum(log_total - picked), logits)


def big_product(left, right):
    return jnp.dot(left, right, preferred_element_type=f32)


def left_product(left, right):
    return lax.dot_general(left, right, (((0,), (0,)), ((), ())), preferred_element_type=f32)


def right_product(left, right):
    return lax.dot_general(left, right, (((1,), (1,)), ((), ())), preferred_element_type=f32)


def combine_parts(first, second):
    new_peak = jnp.maximum(first[0], second[0])
    first_scale = jnp.exp(first[0] - new_peak)
    second_scale = jnp.exp(second[0] - new_peak)
    return (
        new_peak,
        first[1] * first_scale + second[1] * second_scale,
        first[2] * first_scale[..., None] + second[2] * second_scale[..., None],
    )


def nt(left, right, precision=None):
    return lax.dot_general(left, right, (((1,), (1,)), ((), ())), precision=precision, preferred_element_type=f32)


def forward_kernel(heads, query_ref, whole_ref, row_seg_ref, col_seg_ref, context_ref, log_ref):
    width = heads * HEAD_DIM
    rows = query_ref.shape[0]
    same = col_seg_ref[...] == row_seg_ref[...]
    lane = lax.broadcasted_iota(jnp.int32, (rows, 128), 1)
    logs = jnp.zeros((rows, 128), f32)
    pieces = []
    for h in range(heads):
        query = query_ref[:, h * HEAD_DIM : (h + 1) * HEAD_DIM] * jnp.asarray(HEAD_DIM ** (-0.5), bf16)
        key = whole_ref[:, width + h * HEAD_DIM : width + (h + 1) * HEAD_DIM]
        value = whole_ref[:, 2 * width + h * HEAD_DIM : 2 * width + (h + 1) * HEAD_DIM]
        scores = jnp.where(same, nt(query, key), masked_value)
        peak = jnp.max(scores, axis=1, keepdims=True)
        exponent = jnp.exp(scores - peak)
        total = jnp.sum(exponent, axis=1, keepdims=True)
        context = jnp.dot(exponent.astype(bf16), value, preferred_element_type=f32)
        pieces.append((context / total).astype(bf16))
        logs = jnp.where(lane == h, peak + jnp.log(total), logs)
    context_ref[...] = jnp.concatenate(pieces, axis=1)
    log_ref[...] = jnp.transpose(logs)[:8]


def attention_forward(projected, segments, rows=512):
    tokens, triple = projected.shape
    width = triple // 3
    heads = width // HEAD_DIM
    return pl.pallas_call(
        functools.partial(forward_kernel, heads),
        grid=(tokens // rows,),
        in_specs=[
            pl.BlockSpec((rows, triple), lambda i: (i, 0)),
            pl.BlockSpec((tokens, triple), lambda i: (0, 0)),
            pl.BlockSpec((1, tokens), lambda i: (0, 0)),
            pl.BlockSpec((rows, 1), lambda i: (i, 0)),
        ],
        out_specs=[
            pl.BlockSpec((rows, width), lambda i: (i, 0)),
            pl.BlockSpec((8, rows), lambda i: (0, i)),
        ],
        out_shape=[
            jax.ShapeDtypeStruct((tokens, width), bf16),
            jax.ShapeDtypeStruct((8, tokens), f32),
        ],
        cost_estimate=pl.CostEstimate(flops=4 * tokens * tokens * 256 * heads, transcendentals=tokens * tokens * heads, bytes_accessed=10 * tokens * triple),
        name="attention_forward",
    )(projected, projected, segments[None, :], segments[:, None])


def backward_kernel(heads, chunk, first, last, *refs):
    width = heads * HEAD_DIM
    part_ref, whole_ref, grad_ref, context_ref, log_ref, row_seg_ref, col_seg_ref = refs[:7]
    if first:
        query_ref, key_out, value_out, key_total, value_total = refs[7:]
    else:
        key_in, value_in, query_ref, key_out, value_out, key_total, value_total = refs[7:]
    rows = grad_ref.shape[0]
    tokens = whole_ref.shape[0]
    step = pl.program_id(0)

    @pl.when(step == 0)
    def _():
        if first:
            key_total[...] = jnp.zeros_like(key_total)
            value_total[...] = jnp.zeros_like(value_total)
        else:
            key_total[...] = key_in[...]
            value_total[...] = value_in[...]

    scale = HEAD_DIM ** (-0.5)
    row_seg = row_seg_ref[...]
    pieces = []
    for h in range(heads):
        cut = slice(h * HEAD_DIM, (h + 1) * HEAD_DIM)
        query = part_ref[:, cut] * jnp.asarray(scale, bf16)
        grad = grad_ref[:, cut]
        inner = nt(
            jnp.ones((8, HEAD_DIM), f32),
            grad.astype(f32) * context_ref[:, cut].astype(f32),
            highest,
        )[:1]
        log_row = log_ref[h : h + 1, :]
        grad_query = jnp.zeros((rows, HEAD_DIM), f32)
        for c in range(tokens // chunk):
            span = slice(c * chunk, (c + 1) * chunk)
            key = whole_ref[span, width + h * HEAD_DIM : width + (h + 1) * HEAD_DIM]
            value = whole_ref[span, 2 * width + h * HEAD_DIM : 2 * width + (h + 1) * HEAD_DIM]
            same = col_seg_ref[span, :] == row_seg
            soft = jnp.exp(jnp.where(same, nt(key, query) - log_row, masked_value))
            grad_scores = (soft * (nt(value, grad) - inner)).astype(bf16)
            value_total[h, span, :] += jnp.dot(soft.astype(bf16), grad, preferred_element_type=f32)
            key_total[h, span, :] += jnp.dot(grad_scores, query, preferred_element_type=f32)
            grad_query += lax.dot_general(
                grad_scores, key, (((0,), (0,)), ((), ())), preferred_element_type=f32
            )
        pieces.append((grad_query * scale).astype(bf16))
    query_ref[...] = jnp.concatenate(pieces, axis=1)

    @pl.when(step == pl.num_programs(0) - 1)
    def _():
        if last:
            for total, out in ((key_total, key_out), (value_total, value_out)):
                out[...] = jnp.concatenate([total[h].astype(bf16) for h in range(heads)], axis=1)
        else:
            key_out[...] = key_total[...]
            value_out[...] = value_total[...]


def attention_backward(
    projected, segments, logs, context, grad_context, totals, start, calls, rows=256, chunk=768
):
    tokens, triple = projected.shape
    width = triple // 3
    heads = width // HEAD_DIM
    steps = tokens // rows // calls
    base = start * steps
    first, last = start == 0, start == calls - 1
    whole = pl.BlockSpec((heads, tokens, HEAD_DIM), lambda i: (0, 0, 0))
    in_specs = [
        pl.BlockSpec((rows, triple), lambda i: (i + base, 0)),
        pl.BlockSpec((tokens, triple), lambda i: (0, 0)),
        pl.BlockSpec((rows, width), lambda i: (i + base, 0)),
        pl.BlockSpec((rows, width), lambda i: (i + base, 0)),
        pl.BlockSpec((8, rows), lambda i: (0, i + base)),
        pl.BlockSpec((1, rows), lambda i: (0, i + base)),
        pl.BlockSpec((tokens, 1), lambda i: (0, 0)),
    ] + ([] if first else [whole] * 2)
    if last:
        end_spec = pl.BlockSpec((tokens, width), lambda i: (0, 0))
        end_shape = jax.ShapeDtypeStruct((tokens, width), bf16)
    else:
        end_spec = whole
        end_shape = jax.ShapeDtypeStruct((heads, tokens, HEAD_DIM), f32)
    query, key, value = pl.pallas_call(
        functools.partial(backward_kernel, heads, chunk, first, last),
        grid=(steps,),
        in_specs=in_specs,
        out_specs=[pl.BlockSpec((rows, width), lambda i: (i, 0)), end_spec, end_spec],
        out_shape=[jax.ShapeDtypeStruct((steps * rows, width), bf16), end_shape, end_shape],
        scratch_shapes=[pltpu.VMEM((heads, tokens, HEAD_DIM), f32)] * 2,
        cost_estimate=pl.CostEstimate(
            flops=10 * tokens * tokens * 256 * heads // calls,
            transcendentals=tokens * tokens * heads // calls,
            bytes_accessed=14 * tokens * triple,
        ),
        name="attention_backward",
    )(
        projected, projected, grad_context, context, logs,
        segments[None, :], segments[:, None], *(() if first else totals),
    )
    return query, (key, value)


def body(
    hidden_in,
    cotangent,
    lengths,
    slot_order,
    labels,
    w_qkv,
    bias_query,
    bias_value,
    w_out,
    bias_out,
    gain_attn,
    shift_attn,
    w_up,
    bias_up,
    w_down,
    bias_down,
    gain_ffn,
    shift_ffn,
    w_student,
    bias_student,
    pool_query,
    w_pool,
    bias_pool,
    w_class,
    bias_class,
):
    seq_count = lax.axis_size("seq")
    fsdp_count = lax.axis_size("fsdp")
    seq_index = lax.axis_index("seq")
    chip = seq_index // 2
    core = seq_index % 2
    micro = hidden_in.shape[0]
    tokens = hidden_in.shape[2]
    width = hidden_in.shape[3]
    group = slot_order.shape[2]
    docs = lengths.shape[2]
    pool_heads, pool_dim = pool_query.shape
    head_width = width // seq_count
    shard = w_qkv.shape[0]
    first_seq = (seq_index == 0).astype(f32)

    small_list = (
        bias_query,
        bias_value,
        bias_out,
        gain_attn,
        shift_attn,
        bias_down,
        gain_ffn,
        shift_ffn,
    )
    up_rows = bias_up.shape[0] // shard
    student_size = bias_student.shape[0]
    small_all = ring_gather(
        jnp.concatenate(
            [
                jnp.stack(small_list),
                bias_up.reshape(up_rows, shard),
                jnp.pad(bias_student, (0, shard - student_size))[None],
            ]
        )
    ).astype(f32)
    (
        full_bias_query,
        full_bias_value,
        full_bias_out,
        full_gain_attn,
        full_shift_attn,
        full_bias_down,
        full_gain_ffn,
        full_shift_ffn,
    ) = [small_all[:, i].reshape(-1) for i in range(len(small_list))]
    full_bias_up = small_all[:, len(small_list) : -1].reshape(-1)
    full_bias_student = small_all[:, -1, :student_size].reshape(-1)

    own_qkv_shard = lax.dynamic_index_in_dim(
        w_qkv.reshape(shard, 3, seq_count, head_width), seq_index, 2, keepdims=False
    ).reshape(shard, 3 * head_width)
    own_qkv = ring_gather(own_qkv_shard).reshape(width, 3 * head_width)
    own_bias = jnp.concatenate(
        [
            lax.dynamic_slice_in_dim(full_bias_query, seq_index * head_width, head_width),
            jnp.zeros((head_width,), f32),
            lax.dynamic_slice_in_dim(full_bias_value, seq_index * head_width, head_width),
        ]
    )

    hidden = hidden_in[:, 0]
    full_hidden = []
    for m in range(micro):
        both = pair_stack(hidden[m], 2, chip, 0)
        full_hidden.append(pair_stack(both, 1, core, 1).reshape(group, width))

    own_qkv, full_hidden[0], *later = lax.optimization_barrier(
        (own_qkv, full_hidden[0], w_out, w_up, w_down, w_student)
    )
    full_out, full_up, full_down = [gather_rows(part, core) for part in later[:3]]
    full_student = ring_gather(later[3]).reshape(width, -1)

    segments = [segment_ids(slot_order[m, 0], lengths[m, 0]) for m in range(micro)]

    saved = []
    context_parts = []
    for m in range(micro):
        projected = (big_product(full_hidden[m], own_qkv) + own_bias).astype(bf16)
        context_own, logs = attention_forward(projected, segments[m])
        saved.append((projected, logs, context_own))
        view = context_own.reshape(seq_count, tokens, head_width)
        parts = []
        for mask in range(seq_count):
            part = lax.dynamic_index_in_dim(view, seq_index ^ mask, 0, keepdims=False)
            parts.append(part if mask == 0 else swap(part, mask))
        context_parts.append(jnp.concatenate(parts, axis=1))
    context = jnp.concatenate(context_parts, axis=0)
    out_view = full_out.reshape(seq_count, head_width, width)
    out_turned = jnp.concatenate(
        [
            lax.dynamic_index_in_dim(out_view, seq_index ^ mask, 0, keepdims=False)
            for mask in range(seq_count)
        ],
        axis=0,
    )
    branch = big_product(context, out_turned) + full_bias_out
    hidden_rows = hidden.reshape(micro * tokens, width)
    normed, first_norm_back = jax.vjp(
        layer_norm, hidden_rows.astype(f32) + branch, full_gain_attn, full_shift_attn
    )
    normed_low = normed.astype(bf16)
    upward = big_product(normed_low, full_up) + full_bias_up
    active, gelu_back = jax.vjp(exact_gelu, upward)
    active_low = active.astype(bf16)
    downward = big_product(active_low, full_down) + full_bias_down
    final, second_norm_back = jax.vjp(
        layer_norm, normed + downward, full_gain_ffn, full_shift_ffn
    )
    final_low = final.astype(bf16)

    student = big_product(final_low, full_student) + full_bias_student
    pieces = student.reshape(micro, tokens, pool_heads, pool_dim)
    energy = jnp.sum(pieces * pool_query, axis=-1)
    segment_local = jnp.stack(
        [lax.dynamic_slice_in_dim(part, seq_index * tokens, tokens) for part in segments]
    )
    members = (segment_local[:, :, None] == jnp.arange(docs, dtype=jnp.int32))[..., None]
    local_peak = jnp.max(jnp.where(members, energy[:, :, None, :], masked_value), axis=1)
    local_weights = jnp.exp(
        jnp.where(members, energy[:, :, None, :] - local_peak[:, None], masked_value)
    )
    local_total = jnp.sum(local_weights, axis=1)
    local_accum = jnp.einsum("btnh,bthd->bnhd", local_weights, pieces, precision=highest)
    packed = jnp.concatenate([local_peak[..., None], local_total[..., None], local_accum], axis=-1)
    for mask in (1, 2):
        other = swap(packed, mask)
        peak, total, accum = combine_parts(
            (packed[..., 0], packed[..., 1], packed[..., 2:]),
            (other[..., 0], other[..., 1], other[..., 2:]),
        )
        packed = jnp.concatenate([peak[..., None], total[..., None], accum], axis=-1)
    global_peak, global_total, global_accum = packed[..., 0], packed[..., 1], packed[..., 2:]
    pooled_heads = global_accum / global_total[..., None]
    pooled = pooled_heads.reshape(micro * docs, -1)

    def head_loss(pooled_rows, pool_weight, pool_bias, class_weight, class_bias):
        return classify(
            pooled_rows, pool_weight, pool_bias, class_weight, class_bias, labels.reshape(-1)
        )

    loss_value, head_back, logit_rows = jax.vjp(
        head_loss, pooled, w_pool, bias_pool, w_class, bias_class, has_aux=True
    )
    logits = logit_rows.reshape(micro, 1, docs, -1)
    grad_pooled, grad_wpool, grad_bpool, grad_wclass, grad_bclass = head_back(
        jnp.ones_like(loss_value)
    )
    alpha = (
        jnp.exp(jnp.where(members, energy[:, :, None, :] - global_peak[:, None], masked_value))
        / global_total[:, None]
    )
    grad_heads = grad_pooled.reshape(micro, docs, pool_heads, pool_dim)
    along = jnp.einsum("bthd,bnhd->btnh", pieces, grad_heads, precision=highest)
    baseline = jnp.sum(pooled_heads * grad_heads, axis=-1)
    grad_energy = jnp.sum(alpha * (along - baseline[:, None]), axis=2)
    grad_pieces = (
        jnp.einsum("btnh,bnhd->bthd", alpha, grad_heads, precision=highest)
        + grad_energy[..., None] * pool_query
    )
    grad_pool_query = jnp.einsum("bth,bthd->hd", grad_energy, pieces, precision=highest)
    grad_student = grad_pieces.reshape(micro * tokens, -1).astype(bf16)
    grad_w_student = left_product(final_low, grad_student)
    grad_bias_student = jnp.sum(grad_student.astype(f32), axis=0)

    cotangent_rows = cotangent[:, 0].reshape(micro * tokens, width)
    grad_final = cotangent_rows.astype(f32) + right_product(grad_student, full_student)
    grad_mid, grad_gain_ffn, grad_shift_ffn = second_norm_back(grad_final)
    grad_down = grad_mid.astype(bf16)
    grad_bias_down = jnp.sum(grad_down.astype(f32), axis=0)
    grad_w_down = left_product(active_low, grad_down)
    (grad_upward,) = gelu_back(right_product(grad_down, full_down))
    grad_up = grad_upward.astype(bf16)
    grad_bias_up = jnp.sum(grad_up.astype(f32), axis=0)
    grad_w_up = left_product(normed_low, grad_up)
    grad_normed = grad_mid + right_product(grad_up, full_up)
    grad_res, grad_gain_attn, grad_shift_attn = first_norm_back(grad_normed)
    grad_branch = grad_res.astype(bf16)
    grad_bias_out = jnp.sum(grad_branch.astype(f32), axis=0)
    grad_out_turned = left_product(context, grad_branch).reshape(seq_count, head_width, width)
    grad_w_out = jnp.concatenate(
        by_seq([grad_out_turned[m] for m in range(seq_count)], chip, core), axis=0
    )
    grad_context = right_product(grad_branch, out_turned).astype(bf16)

    down = core_stage(grad_w_down, chip, core)
    up = core_stage(grad_w_up, chip, core)
    out = core_stage(grad_w_out, chip, core)
    grad_own_qkv = None
    grad_bias_own = None
    grad_inputs = []
    calls = 3
    slot = 0
    for m in range(micro):
        rows = grad_context[m * tokens : (m + 1) * tokens]
        parts = []
        for mask in range(seq_count):
            part = rows[:, mask * head_width : (mask + 1) * head_width]
            parts.append(part if mask == 0 else swap(part, mask))
        grad_context_own = jnp.concatenate(by_seq(parts, chip, core), axis=0)
        projected, logs, context_own = saved[m]
        totals = None
        query_parts = []
        for call in range(calls):
            if slot == 0:
                grad_context_own, down, up, out = lax.optimization_barrier(
                    (grad_context_own, down, up, out)
                )
                down = chip_stage(down)
            elif slot == 2:
                grad_context_own, down = lax.optimization_barrier((grad_context_own, down))
                up = chip_stage(up)
                down = small_stages(down)
            elif slot == 4:
                grad_context_own, down, up = lax.optimization_barrier((grad_context_own, down, up))
                out = chip_stage(out)
                up = small_stages(up)
                down = last_stage(down)
            elif slot == 5:
                grad_context_own, down, up, out = lax.optimization_barrier(
                    (grad_context_own, down, up, out)
                )
                out = small_stages(out)
                up = last_stage(up)
            query_part, totals = attention_backward(
                projected, segments[m], logs, context_own, grad_context_own, totals, call, calls
            )
            query_parts.append(query_part)
            slot += 1
        grad_proj = jnp.concatenate([jnp.concatenate(query_parts, axis=0), *totals], axis=1)
        bias_sum = jnp.sum(grad_proj.astype(f32), axis=0)
        weight_sum = left_product(full_hidden[m], grad_proj)
        grad_bias_own = bias_sum if grad_bias_own is None else grad_bias_own + bias_sum
        grad_own_qkv = weight_sum if grad_own_qkv is None else grad_own_qkv + weight_sum
        partial = right_product(grad_proj, own_qkv).reshape(2, 2, tokens, width)
        sent = lax.dynamic_index_in_dim(partial, 1 - core, 1, keepdims=False).astype(bf16)
        kept = lax.dynamic_index_in_dim(partial, core, 1, keepdims=False)
        kept = kept + swap(sent, 1).astype(f32)
        sent = lax.dynamic_index_in_dim(kept, 1 - chip, 0, keepdims=False).astype(bf16)
        kept = lax.dynamic_index_in_dim(kept, chip, 0, keepdims=False)
        kept = kept + swap(sent, 2).astype(f32)
        grad_inputs.append(grad_res[m * tokens : (m + 1) * tokens] + kept)

    out = last_stage(out)
    out_w_down = collect(down, chip, core)
    out_w_up = collect(up, chip, core)
    out_w_out = collect(out, chip, core)
    owned_qkv = ring_scatter(grad_own_qkv.reshape(fsdp_count, shard, 3 * head_width)).astype(bf16)
    both = pair_stack(owned_qkv.reshape(shard, 3, head_width), 2, chip, 2)
    out_w_qkv = pair_stack(both, 1, core, 3).reshape(shard, 3 * width).astype(f32)

    early = (
        grad_bias_out,
        grad_gain_attn,
        grad_shift_attn,
        grad_bias_up,
        grad_bias_down,
        grad_gain_ffn,
        grad_shift_ffn,
        grad_bias_student,
        grad_w_student.reshape(-1),
    )
    early_packed = jnp.concatenate([part.reshape(fsdp_count, -1) for part in early], axis=1)
    early_owned = ring_scatter(seq_sum(early_packed, bf16))
    placed_bias = jnp.zeros((2, seq_count, head_width), f32)
    placed_bias = lax.dynamic_update_slice(
        placed_bias,
        grad_bias_own.reshape(3, 1, head_width)[::2],
        (0, seq_index, 0),
    ).reshape(2, fsdp_count, -1)
    late_packed = jnp.concatenate([placed_bias[0], placed_bias[1]], axis=1)
    late_owned = ring_scatter(seq_sum(late_packed), f32)
    early_out = []
    start = 0
    for part in early:
        size = part.size // fsdp_count
        early_out.append(early_owned[start : start + size])
        start += size
    bias_size = late_owned.shape[0] // 2

    query_total = seq_sum(grad_pool_query)
    head_list = (query_total, grad_wpool, grad_bpool, grad_wclass, grad_bclass)
    head_packed = ring_sum(jnp.concatenate([part.reshape(-1) for part in head_list]))
    head_out = []
    start = 0
    for part in head_list:
        head_out.append(head_packed[start : start + part.size].reshape(part.shape))
        start += part.size

    return (
        final_low.reshape(micro, 1, tokens, width),
        logits,
        jnp.stack(grad_inputs)[:, None],
        out_w_qkv,
        late_owned[:bias_size],
        late_owned[bias_size:],
        out_w_out,
        early_out[0],
        early_out[1],
        early_out[2],
        out_w_up,
        early_out[3],
        out_w_down,
        early_out[4],
        early_out[5],
        early_out[6],
        early_out[8].reshape(w_student.shape),
        early_out[7],
    ) + tuple(head_out)


def solution(mesh):
    rows, vector = P("fsdp", None), P("fsdp")
    sharded = (
        rows, vector, vector, rows, vector, vector, vector, rows,
        vector, rows, vector, vector, vector, rows, vector,
    )
    return jax.shard_map(
        body,
        mesh=mesh,
        in_specs=(P(None, "fsdp", "seq", None),) * 2
        + (P(None, "fsdp", None),) * 3
        + sharded
        + (P(),) * 5,
        out_specs=(
            P(None, "fsdp", "seq", None),
            P(None, "fsdp", None, None),
            P(None, "fsdp", "seq", None),
        )
        + sharded
        + (P(),) * 5,
        check_vma=False,
    )
```

```python
import functools

import jax
import jax.numpy as jnp
from jax import lax
from jax.experimental import pallas as pl
from jax.experimental.pallas import tpu as pltpu
from jax.sharding import PartitionSpec as P

HEAD_DIM = 64
highest = lax.Precision.HIGHEST
masked_value = -1e30
bf16 = jnp.bfloat16
f32 = jnp.float32


def factors(count):
    found = []
    while count % 4 == 0:
        found.append(4)
        count //= 4
    if count > 1:
        found.append(count)
    return sorted(found)


def ring_pairs(count, stride, radix, shift):
    pairs = []
    for source in range(count):
        digit = (source // stride) % radix
        pairs.append((source, source + ((digit + shift) % radix - digit) * stride))
    return pairs


def swap(value, mask):
    count = lax.axis_size("seq")
    return lax.ppermute(value, "seq", [(i, i ^ mask) for i in range(count)])


def pair_stack(value, mask, bit, axis):
    other = swap(value, mask)
    return jnp.stack([jnp.where(bit == 0, value, other), jnp.where(bit == 0, other, value)], axis)


def strides(count):
    found = []
    stride = 1
    for radix in factors(count):
        found.append((radix, stride))
        stride *= radix
    return found


def digit_gather(total, radix, stride, axis):
    count = lax.axis_size("fsdp")
    digit = (lax.axis_index("fsdp") // stride) % radix
    parts = [total] + [
        lax.ppermute(total, "fsdp", ring_pairs(count, stride, radix, shift))
        for shift in range(1, radix)
    ]
    if radix == 2:
        return jnp.stack(
            [jnp.where(digit == 0, parts[0], parts[1]), jnp.where(digit == 0, parts[1], parts[0])],
            axis,
        )
    shape = total.shape[:axis] + (radix,) + total.shape[axis:]
    stacked = jnp.zeros(shape, total.dtype)
    for shift, part in enumerate(parts):
        stacked = lax.dynamic_update_index_in_dim(
            stacked, part, lax.rem(digit - shift + radix, radix), axis
        )
    return stacked


def ring_gather(value):
    total = value[None]
    for radix, stride in reversed(strides(lax.axis_size("fsdp"))):
        total = digit_gather(total, radix, stride, 1)
        total = total.reshape((-1,) + value.shape)
    return total


def digit_scatter(value, radix, stride, wire):
    count = lax.axis_size("fsdp")
    digit = (lax.axis_index("fsdp") // stride) % radix
    view = value.reshape((value.shape[0] // radix, radix) + value.shape[1:])

    def piece(offset):
        return lax.dynamic_index_in_dim(view, lax.rem(digit + offset, radix), 1, keepdims=False)

    total = piece(0)
    for shift in range(1, radix):
        moved = lax.ppermute(
            piece(shift).astype(wire), "fsdp", ring_pairs(count, stride, radix, shift)
        )
        total = total + moved.astype(f32)
    return total


def ring_scatter(value, wire=bf16):
    for radix, stride in strides(lax.axis_size("fsdp")):
        value = digit_scatter(value, radix, stride, wire)
    return value[0]


def ring_sum(value):
    for radix, stride in strides(lax.axis_size("fsdp")):
        value = jnp.sum(digit_gather(value, radix, stride, 0), axis=0)
    return value


def seq_sum(value, wire=f32):
    value = value + swap(value.astype(wire), 1).astype(f32)
    return value + swap(value.astype(wire), 2).astype(f32)


def by_seq(parts, chip, core):
    first = [
        jnp.where(core == 0, parts[0], parts[1]),
        jnp.where(core == 0, parts[1], parts[0]),
        jnp.where(core == 0, parts[2], parts[3]),
        jnp.where(core == 0, parts[3], parts[2]),
    ]
    return [
        jnp.where(chip == 0, first[0], first[2]),
        jnp.where(chip == 0, first[1], first[3]),
        jnp.where(chip == 0, first[2], first[0]),
        jnp.where(chip == 0, first[3], first[1]),
    ]


def gather_rows(shard, core):
    rows, columns = shard.shape
    half = rows // 2
    mine = lax.dynamic_slice_in_dim(shard, core * half, half)
    gathered = ring_gather(mine)
    return pair_stack(gathered, 1, core, 1).reshape(-1, columns)


def core_stage(grad, chip, core):
    rows, columns = grad.shape
    count = lax.axis_size("fsdp")
    half = rows // (2 * count)
    wide = columns // 2
    view = grad.reshape(count, 2, half, columns)
    other = lax.dynamic_index_in_dim(view, 1 - core, 1, keepdims=False).astype(bf16)
    total = lax.dynamic_index_in_dim(view, core, 1, keepdims=False) + swap(other, 1).astype(f32)
    low, high = total[..., :wide], total[..., wide:]
    return jnp.where(chip == 0, low, high), jnp.where(chip == 0, high, low).astype(bf16)


def chip_stage(pair):
    kept, sent = pair
    return kept + swap(sent, 2).astype(f32)


def collect(owned, chip, core):
    both = pair_stack(owned.astype(bf16), 2, chip, 0)
    both = jnp.concatenate([both[0], both[1]], axis=-1)
    return pair_stack(both, 1, core, 0).reshape(-1, both.shape[-1]).astype(f32)


def small_stages(value):
    for radix, stride in strides(lax.axis_size("fsdp"))[:-1]:
        value = digit_scatter(value, radix, stride, bf16)
    return value


def last_stage(value):
    radix, stride = strides(lax.axis_size("fsdp"))[-1]
    return digit_scatter(value, radix, stride, bf16)[0]


def layer_norm(values, gain, shift):
    center = values - jnp.mean(values, axis=-1, keepdims=True)
    spread = jnp.mean(center * center, axis=-1, keepdims=True)
    return center * lax.rsqrt(spread + 1e-06) * gain + shift


def exact_gelu(values):
    return jax.nn.gelu(values, approximate=False)


def segment_ids(order_row, length_row):
    ends = jnp.cumsum(length_row)
    above = (order_row[:, None] >= ends[None, :-1]).astype(jnp.int32)
    return jnp.sum(above, axis=1)


def classify(pooled, w_pool, bias_pool, w_class, bias_class, labels):
    inner = jnp.tanh(
        jnp.dot(pooled, w_pool, precision=highest, preferred_element_type=f32) + bias_pool
    )
    logits = jnp.dot(inner, w_class, precision=highest, preferred_element_type=f32) + bias_class
    row_peak = jnp.max(logits, axis=-1, keepdims=True)
    log_total = row_peak[:, 0] + jnp.log(jnp.sum(jnp.exp(logits - row_peak), axis=-1))
    classes = jnp.arange(logits.shape[1])
    picked = jnp.sum(jnp.where(classes[None, :] == labels[:, None], logits, 0.0), axis=-1)
    return (jnp.sum(log_total - picked), logits)


def big_product(left, right):
    return jnp.dot(left, right, preferred_element_type=f32)


def left_product(left, right):
    return lax.dot_general(left, right, (((0,), (0,)), ((), ())), preferred_element_type=f32)


def right_product(left, right):
    return lax.dot_general(left, right, (((1,), (1,)), ((), ())), preferred_element_type=f32)


def combine_parts(first, second):
    new_peak = jnp.maximum(first[0], second[0])
    first_scale = jnp.exp(first[0] - new_peak)
    second_scale = jnp.exp(second[0] - new_peak)
    return (
        new_peak,
        first[1] * first_scale + second[1] * second_scale,
        first[2] * first_scale[..., None] + second[2] * second_scale[..., None],
    )


def nt(left, right, precision=None):
    return lax.dot_general(left, right, (((1,), (1,)), ((), ())), precision=precision, preferred_element_type=f32)


def forward_kernel(heads, query_ref, whole_ref, row_seg_ref, col_seg_ref, context_ref, log_ref):
    width = heads * HEAD_DIM
    rows = query_ref.shape[0]
    same = col_seg_ref[...] == row_seg_ref[...]
    lane = lax.broadcasted_iota(jnp.int32, (rows, 128), 1)
    logs = jnp.zeros((rows, 128), f32)
    pieces = []
    for h in range(heads):
        query = query_ref[:, h * HEAD_DIM : (h + 1) * HEAD_DIM] * jnp.asarray(HEAD_DIM ** (-0.5), bf16)
        key = whole_ref[:, width + h * HEAD_DIM : width + (h + 1) * HEAD_DIM]
        value = whole_ref[:, 2 * width + h * HEAD_DIM : 2 * width + (h + 1) * HEAD_DIM]
        scores = jnp.where(same, nt(query, key), masked_value)
        peak = jnp.max(scores, axis=1, keepdims=True)
        exponent = jnp.exp(scores - peak)
        total = jnp.sum(exponent, axis=1, keepdims=True)
        context = jnp.dot(exponent.astype(bf16), value, preferred_element_type=f32)
        pieces.append((context / total).astype(bf16))
        logs = jnp.where(lane == h, peak + jnp.log(total), logs)
    context_ref[...] = jnp.concatenate(pieces, axis=1)
    log_ref[...] = jnp.transpose(logs)[:8]


def attention_forward(projected, segments, rows=512):
    tokens, triple = projected.shape
    width = triple // 3
    heads = width // HEAD_DIM
    return pl.pallas_call(
        functools.partial(forward_kernel, heads),
        grid=(tokens // rows,),
        in_specs=[
            pl.BlockSpec((rows, triple), lambda i: (i, 0)),
            pl.BlockSpec((tokens, triple), lambda i: (0, 0)),
            pl.BlockSpec((1, tokens), lambda i: (0, 0)),
            pl.BlockSpec((rows, 1), lambda i: (i, 0)),
        ],
        out_specs=[
            pl.BlockSpec((rows, width), lambda i: (i, 0)),
            pl.BlockSpec((8, rows), lambda i: (0, i)),
        ],
        out_shape=[
            jax.ShapeDtypeStruct((tokens, width), bf16),
            jax.ShapeDtypeStruct((8, tokens), f32),
        ],
        cost_estimate=pl.CostEstimate(flops=4 * tokens * tokens * 256 * heads, transcendentals=tokens * tokens * heads, bytes_accessed=10 * tokens * triple),
        name="attention_forward",
    )(projected, projected, segments[None, :], segments[:, None])


def backward_kernel(heads, chunk, first, last, *refs):
    width = heads * HEAD_DIM
    part_ref, whole_ref, grad_ref, context_ref, log_ref, row_seg_ref, col_seg_ref = refs[:7]
    if first:
        query_ref, key_out, value_out, key_total, value_total = refs[7:]
    else:
        key_in, value_in, query_ref, key_out, value_out, key_total, value_total = refs[7:]
    rows = grad_ref.shape[0]
    tokens = whole_ref.shape[0]
    step = pl.program_id(0)

    @pl.when(step == 0)
    def _():
        if first:
            key_total[...] = jnp.zeros_like(key_total)
            value_total[...] = jnp.zeros_like(value_total)
        else:
            key_total[...] = key_in[...]
            value_total[...] = value_in[...]

    scale = HEAD_DIM ** (-0.5)
    row_seg = row_seg_ref[...]
    pieces = []
    for h in range(heads):
        cut = slice(h * HEAD_DIM, (h + 1) * HEAD_DIM)
        query = part_ref[:, cut] * jnp.asarray(scale, bf16)
        grad = grad_ref[:, cut]
        inner = nt(
            jnp.ones((8, HEAD_DIM), f32),
            grad.astype(f32) * context_ref[:, cut].astype(f32),
            highest,
        )[:1]
        log_row = log_ref[h : h + 1, :]
        grad_query = jnp.zeros((rows, HEAD_DIM), f32)
        for c in range(tokens // chunk):
            span = slice(c * chunk, (c + 1) * chunk)
            key = whole_ref[span, width + h * HEAD_DIM : width + (h + 1) * HEAD_DIM]
            value = whole_ref[span, 2 * width + h * HEAD_DIM : 2 * width + (h + 1) * HEAD_DIM]
            same = col_seg_ref[span, :] == row_seg
            soft = jnp.exp(jnp.where(same, nt(key, query) - log_row, masked_value))
            grad_scores = (soft * (nt(value, grad) - inner)).astype(bf16)
            value_total[h, span, :] += jnp.dot(soft.astype(bf16), grad, preferred_element_type=f32)
            key_total[h, span, :] += jnp.dot(grad_scores, query, preferred_element_type=f32)
            grad_query += lax.dot_general(
                grad_scores, key, (((0,), (0,)), ((), ())), preferred_element_type=f32
            )
        pieces.append((grad_query * scale).astype(bf16))
    query_ref[...] = jnp.concatenate(pieces, axis=1)

    @pl.when(step == pl.num_programs(0) - 1)
    def _():
        if last:
            for total, out in ((key_total, key_out), (value_total, value_out)):
                out[...] = jnp.concatenate([total[h].astype(bf16) for h in range(heads)], axis=1)
        else:
            key_out[...] = key_total[...]
            value_out[...] = value_total[...]


def attention_backward(
    projected, segments, logs, context, grad_context, totals, start, calls, rows=256, chunk=768
):
    tokens, triple = projected.shape
    width = triple // 3
    heads = width // HEAD_DIM
    steps = tokens // rows // calls
    base = start * steps
    first, last = start == 0, start == calls - 1
    whole = pl.BlockSpec((heads, tokens, HEAD_DIM), lambda i: (0, 0, 0))
    in_specs = [
        pl.BlockSpec((rows, triple), lambda i: (i + base, 0)),
        pl.BlockSpec((tokens, triple), lambda i: (0, 0)),
        pl.BlockSpec((rows, width), lambda i: (i + base, 0)),
        pl.BlockSpec((rows, width), lambda i: (i + base, 0)),
        pl.BlockSpec((8, rows), lambda i: (0, i + base)),
        pl.BlockSpec((1, rows), lambda i: (0, i + base)),
        pl.BlockSpec((tokens, 1), lambda i: (0, 0)),
    ] + ([] if first else [whole] * 2)
    if last:
        end_spec = pl.BlockSpec((tokens, width), lambda i: (0, 0))
        end_shape = jax.ShapeDtypeStruct((tokens, width), bf16)
    else:
        end_spec = whole
        end_shape = jax.ShapeDtypeStruct((heads, tokens, HEAD_DIM), f32)
    query, key, value = pl.pallas_call(
        functools.partial(backward_kernel, heads, chunk, first, last),
        grid=(steps,),
        in_specs=in_specs,
        out_specs=[pl.BlockSpec((rows, width), lambda i: (i, 0)), end_spec, end_spec],
        out_shape=[jax.ShapeDtypeStruct((steps * rows, width), bf16), end_shape, end_shape],
        scratch_shapes=[pltpu.VMEM((heads, tokens, HEAD_DIM), f32)] * 2,
        cost_estimate=pl.CostEstimate(
            flops=10 * tokens * tokens * 256 * heads // calls,
            transcendentals=tokens * tokens * heads // calls,
            bytes_accessed=14 * tokens * triple,
        ),
        name="attention_backward",
    )(
        projected, projected, grad_context, context, logs,
        segments[None, :], segments[:, None], *(() if first else totals),
    )
    return query, (key, value)


def body(
    hidden_in,
    cotangent,
    lengths,
    slot_order,
    labels,
    w_qkv,
    bias_query,
    bias_value,
    w_out,
    bias_out,
    gain_attn,
    shift_attn,
    w_up,
    bias_up,
    w_down,
    bias_down,
    gain_ffn,
    shift_ffn,
    w_student,
    bias_student,
    pool_query,
    w_pool,
    bias_pool,
    w_class,
    bias_class,
):
    seq_count = lax.axis_size("seq")
    fsdp_count = lax.axis_size("fsdp")
    seq_index = lax.axis_index("seq")
    chip = seq_index // 2
    core = seq_index % 2
    micro = hidden_in.shape[0]
    tokens = hidden_in.shape[2]
    width = hidden_in.shape[3]
    group = slot_order.shape[2]
    docs = lengths.shape[2]
    pool_heads, pool_dim = pool_query.shape
    head_width = width // seq_count
    shard = w_qkv.shape[0]
    first_seq = (seq_index == 0).astype(f32)

    small_list = (
        bias_query,
        bias_value,
        bias_out,
        gain_attn,
        shift_attn,
        bias_down,
        gain_ffn,
        shift_ffn,
    )
    up_rows = bias_up.shape[0] // shard
    student_size = bias_student.shape[0]
    small_all = ring_gather(
        jnp.concatenate(
            [
                jnp.stack(small_list),
                bias_up.reshape(up_rows, shard),
                jnp.pad(bias_student, (0, shard - student_size))[None],
            ]
        )
    ).astype(f32)
    (
        full_bias_query,
        full_bias_value,
        full_bias_out,
        full_gain_attn,
        full_shift_attn,
        full_bias_down,
        full_gain_ffn,
        full_shift_ffn,
    ) = [small_all[:, i].reshape(-1) for i in range(len(small_list))]
    full_bias_up = small_all[:, len(small_list) : -1].reshape(-1)
    full_bias_student = small_all[:, -1, :student_size].reshape(-1)

    own_qkv_shard = lax.dynamic_index_in_dim(
        w_qkv.reshape(shard, 3, seq_count, head_width), seq_index, 2, keepdims=False
    ).reshape(shard, 3 * head_width)
    own_qkv = ring_gather(own_qkv_shard).reshape(width, 3 * head_width)
    own_bias = jnp.concatenate(
        [
            lax.dynamic_slice_in_dim(full_bias_query, seq_index * head_width, head_width),
            jnp.zeros((head_width,), f32),
            lax.dynamic_slice_in_dim(full_bias_value, seq_index * head_width, head_width),
        ]
    )

    hidden = hidden_in[:, 0]
    full_hidden = []
    for m in range(micro):
        both = pair_stack(hidden[m], 2, chip, 0)
        full_hidden.append(pair_stack(both, 1, core, 1).reshape(group, width))

    own_qkv, student_shard = lax.optimization_barrier((own_qkv, w_student))
    full_out, full_up, full_down = [gather_rows(part, core) for part in (w_out, w_up, w_down)]
    full_student = ring_gather(student_shard).reshape(width, -1)

    segments = [segment_ids(slot_order[m, 0], lengths[m, 0]) for m in range(micro)]

    saved = []
    context_parts = []
    for m in range(micro):
        projected = (big_product(full_hidden[m], own_qkv) + own_bias).astype(bf16)
        context_own, logs = attention_forward(projected, segments[m])
        saved.append((projected, logs, context_own))
        view = context_own.reshape(seq_count, tokens, head_width)
        parts = []
        for mask in range(seq_count):
            part = lax.dynamic_index_in_dim(view, seq_index ^ mask, 0, keepdims=False)
            parts.append(part if mask == 0 else swap(part, mask))
        context_parts.append(jnp.concatenate(parts, axis=1))
    context = jnp.concatenate(context_parts, axis=0)
    out_view = full_out.reshape(seq_count, head_width, width)
    out_turned = jnp.concatenate(
        [
            lax.dynamic_index_in_dim(out_view, seq_index ^ mask, 0, keepdims=False)
            for mask in range(seq_count)
        ],
        axis=0,
    )
    branch = big_product(context, out_turned) + full_bias_out
    hidden_rows = hidden.reshape(micro * tokens, width)
    normed, first_norm_back = jax.vjp(
        layer_norm, hidden_rows.astype(f32) + branch, full_gain_attn, full_shift_attn
    )
    normed_low = normed.astype(bf16)
    upward = big_product(normed_low, full_up) + full_bias_up
    active, gelu_back = jax.vjp(exact_gelu, upward)
    active_low = active.astype(bf16)
    downward = big_product(active_low, full_down) + full_bias_down
    final, second_norm_back = jax.vjp(
        layer_norm, normed + downward, full_gain_ffn, full_shift_ffn
    )
    final_low = final.astype(bf16)

    student = big_product(final_low, full_student) + full_bias_student
    pieces = student.reshape(micro, tokens, pool_heads, pool_dim)
    energy = jnp.sum(pieces * pool_query, axis=-1)
    segment_local = jnp.stack(
        [lax.dynamic_slice_in_dim(part, seq_index * tokens, tokens) for part in segments]
    )
    members = (segment_local[:, :, None] == jnp.arange(docs, dtype=jnp.int32))[..., None]
    local_peak = jnp.max(jnp.where(members, energy[:, :, None, :], masked_value), axis=1)
    local_weights = jnp.exp(
        jnp.where(members, energy[:, :, None, :] - local_peak[:, None], masked_value)
    )
    local_total = jnp.sum(local_weights, axis=1)
    local_accum = jnp.einsum("btnh,bthd->bnhd", local_weights, pieces, precision=highest)
    packed = jnp.concatenate([local_peak[..., None], local_total[..., None], local_accum], axis=-1)
    for mask in (1, 2):
        other = swap(packed, mask)
        peak, total, accum = combine_parts(
            (packed[..., 0], packed[..., 1], packed[..., 2:]),
            (other[..., 0], other[..., 1], other[..., 2:]),
        )
        packed = jnp.concatenate([peak[..., None], total[..., None], accum], axis=-1)
    global_peak, global_total, global_accum = packed[..., 0], packed[..., 1], packed[..., 2:]
    pooled_heads = global_accum / global_total[..., None]
    pooled = pooled_heads.reshape(micro * docs, -1)

    def head_loss(pooled_rows, pool_weight, pool_bias, class_weight, class_bias):
        return classify(
            pooled_rows, pool_weight, pool_bias, class_weight, class_bias, labels.reshape(-1)
        )

    loss_value, head_back, logit_rows = jax.vjp(
        head_loss, pooled, w_pool, bias_pool, w_class, bias_class, has_aux=True
    )
    logits = logit_rows.reshape(micro, 1, docs, -1)
    grad_pooled, grad_wpool, grad_bpool, grad_wclass, grad_bclass = head_back(
        jnp.ones_like(loss_value)
    )
    alpha = (
        jnp.exp(jnp.where(members, energy[:, :, None, :] - global_peak[:, None], masked_value))
        / global_total[:, None]
    )
    grad_heads = grad_pooled.reshape(micro, docs, pool_heads, pool_dim)
    along = jnp.einsum("bthd,bnhd->btnh", pieces, grad_heads, precision=highest)
    baseline = jnp.sum(pooled_heads * grad_heads, axis=-1)
    grad_energy = jnp.sum(alpha * (along - baseline[:, None]), axis=2)
    grad_pieces = (
        jnp.einsum("btnh,bnhd->bthd", alpha, grad_heads, precision=highest)
        + grad_energy[..., None] * pool_query
    )
    grad_pool_query = jnp.einsum("bth,bthd->hd", grad_energy, pieces, precision=highest)
    grad_student = grad_pieces.reshape(micro * tokens, -1).astype(bf16)
    grad_w_student = left_product(final_low, grad_student)
    grad_bias_student = jnp.sum(grad_student.astype(f32), axis=0)

    cotangent_rows = cotangent[:, 0].reshape(micro * tokens, width)
    grad_final = cotangent_rows.astype(f32) + right_product(grad_student, full_student)
    grad_mid, grad_gain_ffn, grad_shift_ffn = second_norm_back(grad_final)
    grad_down = grad_mid.astype(bf16)
    grad_bias_down = jnp.sum(grad_down.astype(f32), axis=0)
    grad_w_down = left_product(active_low, grad_down)
    (grad_upward,) = gelu_back(right_product(grad_down, full_down))
    grad_up = grad_upward.astype(bf16)
    grad_bias_up = jnp.sum(grad_up.astype(f32), axis=0)
    grad_w_up = left_product(normed_low, grad_up)
    grad_normed = grad_mid + right_product(grad_up, full_up)
    grad_res, grad_gain_attn, grad_shift_attn = first_norm_back(grad_normed)
    grad_branch = grad_res.astype(bf16)
    grad_bias_out = jnp.sum(grad_branch.astype(f32), axis=0)
    grad_out_turned = left_product(context, grad_branch).reshape(seq_count, head_width, width)
    grad_w_out = jnp.concatenate(
        by_seq([grad_out_turned[m] for m in range(seq_count)], chip, core), axis=0
    )
    grad_context = right_product(grad_branch, out_turned).astype(bf16)

    down = core_stage(grad_w_down, chip, core)
    up = core_stage(grad_w_up, chip, core)
    out = core_stage(grad_w_out, chip, core)
    grad_own_qkv = None
    grad_bias_own = None
    grad_inputs = []
    calls = 3
    slot = 0
    for m in range(micro):
        rows = grad_context[m * tokens : (m + 1) * tokens]
        parts = []
        for mask in range(seq_count):
            part = rows[:, mask * head_width : (mask + 1) * head_width]
            parts.append(part if mask == 0 else swap(part, mask))
        grad_context_own = jnp.concatenate(by_seq(parts, chip, core), axis=0)
        projected, logs, context_own = saved[m]
        totals = None
        query_parts = []
        for call in range(calls):
            if slot == 0:
                grad_context_own, down, up, out = lax.optimization_barrier(
                    (grad_context_own, down, up, out)
                )
                down = chip_stage(down)
            elif slot == 2:
                grad_context_own, down = lax.optimization_barrier((grad_context_own, down))
                up = chip_stage(up)
                down = small_stages(down)
            elif slot == 4:
                grad_context_own, down, up = lax.optimization_barrier((grad_context_own, down, up))
                out = chip_stage(out)
                up = small_stages(up)
                down = last_stage(down)
            elif slot == 5:
                grad_context_own, down, up, out = lax.optimization_barrier(
                    (grad_context_own, down, up, out)
                )
                out = small_stages(out)
                up = last_stage(up)
            query_part, totals = attention_backward(
                projected, segments[m], logs, context_own, grad_context_own, totals, call, calls
            )
            query_parts.append(query_part)
            slot += 1
        grad_proj = jnp.concatenate([jnp.concatenate(query_parts, axis=0), *totals], axis=1)
        bias_sum = jnp.sum(grad_proj.astype(f32), axis=0)
        weight_sum = left_product(full_hidden[m], grad_proj)
        grad_bias_own = bias_sum if grad_bias_own is None else grad_bias_own + bias_sum
        grad_own_qkv = weight_sum if grad_own_qkv is None else grad_own_qkv + weight_sum
        partial = right_product(grad_proj, own_qkv).reshape(2, 2, tokens, width)
        sent = lax.dynamic_index_in_dim(partial, 1 - core, 1, keepdims=False).astype(bf16)
        kept = lax.dynamic_index_in_dim(partial, core, 1, keepdims=False)
        kept = kept + swap(sent, 1).astype(f32)
        sent = lax.dynamic_index_in_dim(kept, 1 - chip, 0, keepdims=False).astype(bf16)
        kept = lax.dynamic_index_in_dim(kept, chip, 0, keepdims=False)
        kept = kept + swap(sent, 2).astype(f32)
        grad_inputs.append(grad_res[m * tokens : (m + 1) * tokens] + kept)

    out = last_stage(out)
    out_w_down = collect(down, chip, core)
    out_w_up = collect(up, chip, core)
    out_w_out = collect(out, chip, core)
    owned_qkv = ring_scatter(grad_own_qkv.reshape(fsdp_count, shard, 3 * head_width)).astype(bf16)
    both = pair_stack(owned_qkv.reshape(shard, 3, head_width), 2, chip, 2)
    out_w_qkv = pair_stack(both, 1, core, 3).reshape(shard, 3 * width).astype(f32)

    early = (
        grad_bias_out,
        grad_gain_attn,
        grad_shift_attn,
        grad_bias_up,
        grad_bias_down,
        grad_gain_ffn,
        grad_shift_ffn,
        grad_bias_student,
        grad_w_student.reshape(-1),
    )
    early_packed = jnp.concatenate([part.reshape(fsdp_count, -1) for part in early], axis=1)
    early_owned = ring_scatter(seq_sum(early_packed, bf16))
    placed_bias = jnp.zeros((2, seq_count, head_width), f32)
    placed_bias = lax.dynamic_update_slice(
        placed_bias,
        grad_bias_own.reshape(3, 1, head_width)[::2],
        (0, seq_index, 0),
    ).reshape(2, fsdp_count, -1)
    late_packed = jnp.concatenate([placed_bias[0], placed_bias[1]], axis=1)
    late_owned = ring_scatter(seq_sum(late_packed), f32)
    early_out = []
    start = 0
    for part in early:
        size = part.size // fsdp_count
        early_out.append(early_owned[start : start + size])
        start += size
    bias_size = late_owned.shape[0] // 2

    query_total = seq_sum(grad_pool_query)
    head_list = (query_total, grad_wpool, grad_bpool, grad_wclass, grad_bclass)
    head_packed = ring_sum(jnp.concatenate([part.reshape(-1) for part in head_list]))
    head_out = []
    start = 0
    for part in head_list:
        head_out.append(head_packed[start : start + part.size].reshape(part.shape))
        start += part.size

    return (
        final_low.reshape(micro, 1, tokens, width),
        logits,
        jnp.stack(grad_inputs)[:, None],
        out_w_qkv,
        late_owned[:bias_size],
        late_owned[bias_size:],
        out_w_out,
        early_out[0],
        early_out[1],
        early_out[2],
        out_w_up,
        early_out[3],
        out_w_down,
        early_out[4],
        early_out[5],
        early_out[6],
        early_out[8].reshape(w_student.shape),
        early_out[7],
    ) + tuple(head_out)


def solution(mesh):
    rows, vector = P("fsdp", None), P("fsdp")
    sharded = (
        rows, vector, vector, rows, vector, vector, vector, rows,
        vector, rows, vector, vector, vector, rows, vector,
    )
    return jax.shard_map(
        body,
        mesh=mesh,
        in_specs=(P(None, "fsdp", "seq", None),) * 2
        + (P(None, "fsdp", None),) * 3
        + sharded
        + (P(),) * 5,
        out_specs=(
            P(None, "fsdp", "seq", None),
            P(None, "fsdp", None, None),
            P(None, "fsdp", "seq", None),
        )
        + sharded
        + (P(),) * 5,
        check_vma=False,
    )
```
